256 devices in a mesh: dp: 8 (over x_hi, y), seq: 32 (over x_lo, z, core).
Axes of the slice: x: 4 (x_hi: 2, x_lo: 2; x = x_hi * 2 + x_lo), y: 4, z: 8, core: 2. Of those that a mesh axis runs over, the one named last changes fastest.
Arguments:
- query_seq: bfloat16 [8, 16384, 256], P('dp', 'seq'), may hold values from -6 to 6
- key_seq: bfloat16 [8, 16384, 256], P('dp', 'seq'), may hold values from -6 to 6
- value_seq: bfloat16 [8, 16384, 256], P('dp', 'seq'), may hold values from -6 to 6
- upstream: bfloat16 [8, 16384, 256], P('dp', 'seq'), may hold values from -6 to 6
- filter_param: float32 [16384, 256], P('seq'), may hold values from -6 to 6
Outputs:
- output: bfloat16 [8, 16384, 256], P('dp', 'seq')
- query_grad: bfloat16 [8, 16384, 256], P('dp', 'seq')
- key_grad: bfloat16 [8, 16384, 256], P('dp', 'seq')
- value_grad: bfloat16 [8, 16384, 256], P('dp', 'seq')
- filter_grad: float32 [16384, 256], P('seq')
The draws below stay inside these ranges and needn't reach their ends.
All inputs are finite; a program needn't handle non-finite values.
Results may differ from the reference program's by a relative error of at most 0.0012.
Values sent between devices are 32-bit elements; how exact they have to be, the bound alone decides.
No kernel may reach another device: no remote copies, remote signals or barrier semaphores. Data moves between devices by JAX's collectives and lax.ppermute only.
A program may use at most 128 MiB of HBM per device.

```python
import math
import jax
import jax.numpy as jnp

C = 256
SEQS = 8
TOKENS = 16384


def block_scale(rng, dims, pieces, least, largest):
    level = 1.0
    for axis_at, blocks in pieces:
        draws = jax.random.uniform(jax.random.fold_in(jax.random.fold_in(rng, 6), axis_at), (blocks,), jnp.float32, least / len(pieces), largest / len(pieces))
        level = level * jnp.repeat(jnp.exp(draws), dims[axis_at] // blocks).reshape((-1,) + (1,) * (len(dims) - 1 - axis_at))
    return level


def gaussian(rng, shape, scale, bound, pieces=(), held_as=jnp.bfloat16):
    result = jax.random.normal(rng, shape, jnp.float32) * scale
    if len(pieces) > 0:
        result = block_scale(rng, shape, pieces, -0.22, 0.18) * result
    return jnp.clip(result, min=-bound, max=bound).astype(held_as)


def setup_inputs(seed: int = 0) -> dict:
    keys = jax.random.split(jax.random.key(seed), 6)
    query_seq = gaussian(keys[0], (SEQS, TOKENS, C), 1.0, 6.0, ((0, 8), (1, 32)))
    key_seq = gaussian(keys[1], (SEQS, TOKENS, C), 1.0, 6.0, ((0, 8), (1, 32)))
    value_seq = gaussian(keys[2], (SEQS, TOKENS, C), 1.0, 6.0, ((0, 8), (1, 32)))
    upstream = gaussian(keys[3], (SEQS, TOKENS, C), 1.0, 6.0, ((0, 8), (1, 32)))
    filter_param = gaussian(keys[4], (TOKENS, C), 1.0, 6.0, ((0, 32),), jnp.float32)
    return dict(query_seq=query_seq, key_seq=key_seq, value_seq=value_seq, upstream=upstream, filter_param=filter_param)


def reference(query_seq, key_seq, value_seq, upstream, filter_param):
    length = query_seq.shape[1]
    norm_factor = 1.0 / math.sqrt(length)
    filt = filter_param * norm_factor
    filt_spec = jnp.fft.fft(filt, n=2 * length, axis=0)
    outputs = []
    query_grads = []
    key_grads = []
    value_grads = []
    filter_total = jnp.zeros(filter_param.shape, jnp.float32)
    for seq_index in range(SEQS):
        query_rows = query_seq[seq_index].astype(jnp.float32)
        key_rows = key_seq[seq_index].astype(jnp.float32)
        value_rows = value_seq[seq_index].astype(jnp.float32)
        grad_rows = upstream[seq_index].astype(jnp.float32)
        mixed = key_rows * value_rows
        gated = grad_rows * query_rows
        mixed_spec = jnp.fft.fft(mixed, n=2 * length, axis=0)
        gated_spec = jnp.fft.fft(gated, n=2 * length, axis=0)
        conv = jnp.real(jnp.fft.ifft(filt_spec * mixed_spec, axis=0))[:length].astype(jnp.float32)
        back = jnp.real(jnp.fft.ifft(jnp.conj(filt_spec) * gated_spec, axis=0))[:length].astype(jnp.float32)
        lagged = jnp.real(jnp.fft.ifft(jnp.conj(mixed_spec) * gated_spec, axis=0))[:length].astype(jnp.float32)
        filter_total = filter_total + lagged
        outputs.append((query_rows * conv).astype(jnp.bfloat16))
        query_grads.append((grad_rows * conv).astype(jnp.bfloat16))
        key_grads.append((back * value_rows).astype(jnp.bfloat16))
        value_grads.append((back * key_rows).astype(jnp.bfloat16))
    filter_grad = filter_total * norm_factor
    return (jnp.stack(outputs), jnp.stack(query_grads), jnp.stack(key_grads), jnp.stack(value_grads), filter_grad)
```

```python
import math

import jax
import jax.numpy as jnp
import ml_dtypes
import numpy as np
from jax import lax
from jax.experimental import pallas as pl
from jax.experimental.pallas import tpu as pltpu
from jax.sharding import PartitionSpec as P

LANES = 128
BLOCK = 512
CHANNELS = 256
SEQS = 8
OWNERS = 32
PIECES = BLOCK // LANES
ROWS_IN = 2 * PIECES + 1
ROWS_OUT = 3 * PIECES
HALF = 128
LENGTH = 2 * BLOCK * OWNERS
VMEM_LIMIT = 56 << 20


def split_parts(values):
    high = values.astype(np.float32).astype(ml_dtypes.bfloat16)
    low = (values - high.astype(np.float64)).astype(np.float32).astype(ml_dtypes.bfloat16)
    return high, low


def constants():
    freq = np.arange(HALF, dtype=np.int64)
    rows = np.arange(HALF, dtype=np.int64)
    coarse = (rows % OWNERS) * PIECES + rows // OWNERS
    turn = 2.0 * np.pi * (np.outer(2 * freq + 1, coarse) % (4 * HALF)) / (4 * HALF)
    outer = np.concatenate([np.cos(turn), -np.sin(turn)], axis=0)
    outer_high, outer_low = split_parts(outer)
    outer_cat = np.concatenate([outer_high, outer_high, outer_low], axis=1)
    scale = 2.0 / LENGTH / math.sqrt(LENGTH // 2)
    back_outer = outer.T * scale
    back_high, back_low = split_parts(back_outer)
    back_cat = np.concatenate([back_high, back_high, back_low], axis=1)
    lanes = np.arange(LANES, dtype=np.int64)
    inner_turn = 2.0 * np.pi * (np.outer(lanes, lanes) % LANES) / LANES
    cos_in, sin_in = np.cos(inner_turn), np.sin(inner_turn)
    inner = np.block([[cos_in, -sin_in], [sin_in, cos_in]])
    inner_high, inner_low = split_parts(inner)
    inner_cat = np.concatenate([inner_high, inner_high, inner_low], axis=0)
    inner_back = np.concatenate([inner_high.T, inner_high.T, inner_low.T], axis=0)
    twist = 2.0 * np.pi * np.outer(2 * freq + 1, lanes) / (2 * LENGTH)
    twiddle = np.stack([np.cos(twist), np.sin(twist)]).astype(np.float32)
    return (outer_cat, inner_cat, inner_back, back_cat, twiddle)


def pre_kernel(part_ref, q_ref, k_ref, v_ref, u_ref, f_ref, out_ref):
    del part_ref
    for piece in range(PIECES):
        at = pl.ds(piece * LANES, LANES)
        mixed = k_ref[0, at, :].astype(jnp.float32) * v_ref[0, at, :].astype(jnp.float32)
        gated = u_ref[0, at, :].astype(jnp.float32) * q_ref[0, at, :].astype(jnp.float32)
        out_ref[pl.ds(piece, CHANNELS, stride=ROWS_IN), :] = mixed.T
        out_ref[pl.ds(PIECES + piece, CHANNELS, stride=ROWS_IN), :] = gated.T
    out_ref[pl.ds(2 * PIECES, CHANNELS, stride=ROWS_IN), :] = f_ref[...].T


def halves(value, axis):
    high = value.astype(jnp.bfloat16)
    low = (value - high.astype(jnp.float32)).astype(jnp.bfloat16)
    return jnp.concatenate([high, low, high], axis=axis)


def dot(left, right):
    return jnp.dot(left, right, preferred_element_type=jnp.float32)


def fft_kernel(in_ref, outer_ref, inner_ref, inner_back_ref, back_ref, twiddle_ref, out_ref):
    cos_t = twiddle_ref[0]
    sin_t = twiddle_ref[1]

    def spectra(signals):
        stacked = halves(jnp.concatenate(signals, axis=1), 0)
        first = dot(outer_ref[...], stacked)
        turned = []
        for index in range(len(signals)):
            at = slice(index * LANES, (index + 1) * LANES)
            real, imag = first[:HALF, at], first[HALF:, at]
            turned.append(
                jnp.concatenate([real * cos_t + imag * sin_t, imag * cos_t - real * sin_t], axis=1)
            )
        return dot(halves(jnp.concatenate(turned, axis=0), 1), inner_ref[...])

    def signals_of(spectrum_list):
        rows = dot(halves(jnp.concatenate(spectrum_list, axis=0), 1), inner_back_ref[...])
        turned = []
        for index in range(len(spectrum_list)):
            at = slice(index * HALF, (index + 1) * HALF)
            real, imag = rows[at, :LANES], rows[at, LANES:]
            turned.append(
                jnp.concatenate([real * cos_t - imag * sin_t, imag * cos_t + real * sin_t], axis=0)
            )
        return dot(back_ref[...], halves(jnp.concatenate(turned, axis=1), 0))

    taps = jnp.concatenate(
        [
            in_ref[pl.ds(2 * piece * OWNERS * ROWS_IN + 2 * PIECES, OWNERS, stride=ROWS_IN), :]
            for piece in range(PIECES)
        ],
        axis=0,
    )
    taps_spec = spectra([taps])
    taps_real, taps_imag = taps_spec[:, :LANES], taps_spec[:, LANES:]
    lag_real = jnp.zeros((HALF, LANES), jnp.float32)
    lag_imag = jnp.zeros((HALF, LANES), jnp.float32)
    for seq in range(SEQS):
        signals = [
            jnp.concatenate(
                [
                    in_ref[pl.ds(seq * OWNERS * ROWS_IN + which * PIECES + piece, OWNERS, stride=ROWS_IN), :]
                    for piece in range(PIECES)
                ],
                axis=0,
            )
            for which in range(2)
        ]
        spec = spectra(signals)
        mixed_real, mixed_imag = spec[:HALF, :LANES], spec[:HALF, LANES:]
        gated_real, gated_imag = spec[HALF:, :LANES], spec[HALF:, LANES:]
        conv = jnp.concatenate(
            [
                taps_real * mixed_real - taps_imag * mixed_imag,
                taps_real * mixed_imag + taps_imag * mixed_real,
            ],
            axis=1,
        )
        back = jnp.concatenate(
            [
                taps_real * gated_real + taps_imag * gated_imag,
                taps_real * gated_imag - taps_imag * gated_real,
            ],
            axis=1,
        )
        lag_real = lag_real + (mixed_real * gated_real + mixed_imag * gated_imag)
        lag_imag = lag_imag + (mixed_real * gated_imag - mixed_imag * gated_real)
        result = signals_of([conv, back])
        for which in range(2):
            for piece in range(PIECES):
                out_ref[
                    pl.ds(seq * OWNERS * ROWS_OUT + which * PIECES + piece, OWNERS, stride=ROWS_OUT), :
                ] = result[piece * OWNERS : (piece + 1) * OWNERS, which * LANES : (which + 1) * LANES]
    lag = signals_of([jnp.concatenate([lag_real, lag_imag], axis=1)])
    for seq in range(SEQS):
        for piece in range(PIECES):
            out_ref[
                pl.ds(seq * OWNERS * ROWS_OUT + 2 * PIECES + piece, OWNERS, stride=ROWS_OUT), :
            ] = lag[piece * OWNERS : (piece + 1) * OWNERS, :]


def post_kernel(c_ref, q_ref, k_ref, v_ref, u_ref, o_ref, qg_ref, kg_ref, vg_ref, fg_ref):
    for piece in range(PIECES):
        at = pl.ds(piece * LANES, LANES)
        conv = c_ref[pl.ds(piece, CHANNELS, stride=ROWS_OUT), :].T
        back = c_ref[pl.ds(PIECES + piece, CHANNELS, stride=ROWS_OUT), :].T
        o_ref[0, at, :] = (q_ref[0, at, :].astype(jnp.float32) * conv).astype(jnp.bfloat16)
        qg_ref[0, at, :] = (u_ref[0, at, :].astype(jnp.float32) * conv).astype(jnp.bfloat16)
        kg_ref[0, at, :] = (back * v_ref[0, at, :].astype(jnp.float32)).astype(jnp.bfloat16)
        vg_ref[0, at, :] = (back * k_ref[0, at, :].astype(jnp.float32)).astype(jnp.bfloat16)
        fg_ref[at, :] = c_ref[pl.ds(2 * PIECES + piece, CHANNELS, stride=ROWS_OUT), :].T


def params():
    return pltpu.CompilerParams(vmem_limit_bytes=VMEM_LIMIT)


def pre(part, query_seq, key_seq, value_seq, upstream, filter_param):
    whole = pl.BlockSpec((1, BLOCK, CHANNELS), lambda i, part: (0, 0, 0))
    return pl.pallas_call(
        pre_kernel,
        out_shape=jax.ShapeDtypeStruct((CHANNELS * ROWS_IN, LANES), jnp.float32),
        grid_spec=pltpu.PrefetchScalarGridSpec(
            num_scalar_prefetch=1,
            grid=(1,),
            in_specs=[whole] * 4 + [pl.BlockSpec((LANES, CHANNELS), lambda i, part: (part[0], 0))],
            out_specs=pl.BlockSpec((CHANNELS * ROWS_IN, LANES), lambda i, part: (0, 0)),
        ),
        compiler_params=params(),
    )(part, query_seq, key_seq, value_seq, upstream, filter_param)


def transform(arrived, tables):
    return pl.pallas_call(
        fft_kernel,
        out_shape=jax.ShapeDtypeStruct((SEQS * OWNERS * ROWS_OUT, LANES), jnp.float32),
        compiler_params=params(),
    )(arrived, *tables)


def post(returned, query_seq, key_seq, value_seq, upstream):
    half = jax.ShapeDtypeStruct((1, BLOCK, CHANNELS), jnp.bfloat16)
    return pl.pallas_call(
        post_kernel,
        out_shape=(half, half, half, half, jax.ShapeDtypeStruct((BLOCK, CHANNELS), jnp.float32)),
        compiler_params=params(),
    )(returned, query_seq, key_seq, value_seq, upstream)


def exchange(rows, depth):
    shaped = rows.reshape(CHANNELS, depth, 1, LANES)
    moved = lax.all_to_all(shaped, ("dp", "seq"), split_axis=0, concat_axis=0, tiled=True)
    return moved.reshape(CHANNELS * depth, LANES)


def local(query_seq, key_seq, value_seq, upstream, filter_param):
    tables = [jnp.asarray(table) for table in constants()]
    part = (lax.axis_index("dp") // 2).astype(jnp.int32).reshape(1)
    sent = pre(part, query_seq, key_seq, value_seq, upstream, filter_param)
    arrived = exchange(sent, ROWS_IN)
    results = transform(arrived, tables)
    returned = exchange(results, ROWS_OUT)
    return post(returned, query_seq, key_seq, value_seq, upstream)


def solution(mesh):
    in_specs = (
        P("dp", "seq", None),
        P("dp", "seq", None),
        P("dp", "seq", None),
        P("dp", "seq", None),
        P("seq", None),
    )
    out_specs = (
        P("dp", "seq", None),
        P("dp", "seq", None),
        P("dp", "seq", None),
        P("dp", "seq", None),
        P("seq", None),
    )
    return jax.shard_map(local, mesh=mesh, in_specs=in_specs, out_specs=out_specs, check_vma=False)
```

```python
import math

import jax
import jax.numpy as jnp
import ml_dtypes
import numpy as np
from jax import lax
from jax.experimental import pallas as pl
from jax.experimental.pallas import tpu as pltpu
from jax.sharding import PartitionSpec as P

LANES = 128
BLOCK = 512
CHANNELS = 256
SEQS = 8
OWNERS = 32
PIECES = BLOCK // LANES
ROWS_IN = 2 * PIECES + 1
ROWS_OUT = 3 * PIECES
HALF = 128
LENGTH = 2 * BLOCK * OWNERS
GROUP = 4
VMEM_LIMIT = 32 << 20


def split_parts(values):
    high = values.astype(np.float32).astype(ml_dtypes.bfloat16)
    low = (values - high.astype(np.float64)).astype(np.float32).astype(ml_dtypes.bfloat16)
    return high, low


def constants():
    freq = np.arange(HALF, dtype=np.int64)
    rows = np.arange(HALF, dtype=np.int64)
    coarse = (rows % OWNERS) * PIECES + rows // OWNERS
    turn = 2.0 * np.pi * (np.outer(2 * freq + 1, coarse) % (4 * HALF)) / (4 * HALF)
    outer = np.concatenate([np.cos(turn), -np.sin(turn)], axis=0)
    outer_high, outer_low = split_parts(outer)
    outer_cat = np.concatenate([outer_high, outer_high, outer_low], axis=1)
    scale = 2.0 / LENGTH / math.sqrt(LENGTH // 2)
    back_outer = outer.T * scale
    back_high, back_low = split_parts(back_outer)
    back_cat = np.concatenate([back_high, back_high, back_low], axis=1)
    lanes = np.arange(LANES, dtype=np.int64)
    inner_turn = 2.0 * np.pi * (np.outer(lanes, lanes) % LANES) / LANES
    cos_in, sin_in = np.cos(inner_turn), np.sin(inner_turn)
    inner = np.block([[cos_in, -sin_in], [sin_in, cos_in]])
    inner_high, inner_low = split_parts(inner)
    inner_cat = np.concatenate([inner_high, inner_high, inner_low], axis=0)
    inner_back = np.concatenate([inner_high.T, inner_high.T, inner_low.T], axis=0)
    twist = 2.0 * np.pi * np.outer(2 * freq + 1, lanes) / (2 * LENGTH)
    twiddle = np.stack([np.cos(twist), np.sin(twist)]).astype(np.float32)
    return (outer_cat, inner_cat, inner_back, back_cat, twiddle)


def pre_kernel(part_ref, q_ref, k_ref, v_ref, u_ref, f_ref, out_ref):
    del part_ref
    for piece in range(PIECES):
        at = pl.ds(piece * LANES, LANES)
        mixed = k_ref[0, at, :].astype(jnp.float32) * v_ref[0, at, :].astype(jnp.float32)
        gated = u_ref[0, at, :].astype(jnp.float32) * q_ref[0, at, :].astype(jnp.float32)
        out_ref[pl.ds(piece, CHANNELS, stride=ROWS_IN), :] = mixed.T
        out_ref[pl.ds(PIECES + piece, CHANNELS, stride=ROWS_IN), :] = gated.T
    out_ref[pl.ds(2 * PIECES, CHANNELS, stride=ROWS_IN), :] = f_ref[...].T


def halves(value, axis):
    high = value.astype(jnp.bfloat16)
    low = (value - high.astype(jnp.float32)).astype(jnp.bfloat16)
    return jnp.concatenate([high, low, high], axis=axis)


def dot(left, right):
    return jnp.dot(left, right, preferred_element_type=jnp.float32)


def fft_kernel(in_ref, outer_ref, inner_ref, inner_back_ref, back_ref, twiddle_ref, out_ref):
    cos_t = twiddle_ref[0]
    sin_t = twiddle_ref[1]

    def load(base):
        return jnp.concatenate(
            [in_ref[pl.ds(base + piece, OWNERS, stride=ROWS_IN), :] for piece in range(PIECES)], axis=0
        )

    def outer(signals):
        first = dot(outer_ref[...], halves(jnp.concatenate(signals, axis=1), 0))
        turned = []
        for index in range(len(signals)):
            at = slice(index * LANES, (index + 1) * LANES)
            real, imag = first[:HALF, at], first[HALF:, at]
            turned.append(
                jnp.concatenate([real * cos_t + imag * sin_t, imag * cos_t - real * sin_t], axis=1)
            )
        return turned

    def inner(blocks, table_ref):
        return dot(halves(jnp.concatenate(blocks, axis=0), 1), table_ref[...])

    def outer_back(rows):
        turned = []
        for index in range(rows.shape[0] // HALF):
            at = slice(index * HALF, (index + 1) * HALF)
            real, imag = rows[at, :LANES], rows[at, LANES:]
            turned.append(
                jnp.concatenate([real * cos_t - imag * sin_t, imag * cos_t + real * sin_t], axis=0)
            )
        return dot(back_ref[...], halves(jnp.concatenate(turned, axis=1), 0))

    def store(result, base):
        for piece in range(PIECES):
            out_ref[pl.ds(base + piece, OWNERS, stride=ROWS_OUT), :] = result[
                piece * OWNERS : (piece + 1) * OWNERS, :
            ]

    taps = jnp.concatenate(
        [
            in_ref[pl.ds(2 * piece * OWNERS * ROWS_IN + 2 * PIECES, OWNERS, stride=ROWS_IN), :]
            for piece in range(PIECES)
        ],
        axis=0,
    )
    lag_real = jnp.zeros((HALF, LANES), jnp.float32)
    lag_imag = jnp.zeros((HALF, LANES), jnp.float32)
    for start in range(0, SEQS, GROUP):
        turned = []
        for seq in range(start, start + GROUP):
            base = seq * OWNERS * ROWS_IN
            turned += outer([load(base), load(base + PIECES)])
        if start == 0:
            turned += outer([taps])
        spec = inner(turned, inner_ref)
        if start == 0:
            taps_real, taps_imag = spec[2 * GROUP * HALF :, :LANES], spec[2 * GROUP * HALF :, LANES:]
        products = []
        for index in range(GROUP):
            at = slice(2 * index * HALF, (2 * index + 1) * HALF)
            mixed_real, mixed_imag = spec[at, :LANES], spec[at, LANES:]
            at = slice((2 * index + 1) * HALF, (2 * index + 2) * HALF)
            gated_real, gated_imag = spec[at, :LANES], spec[at, LANES:]
            products.append(
                jnp.concatenate(
                    [
                        taps_real * mixed_real - taps_imag * mixed_imag,
                        taps_real * mixed_imag + taps_imag * mixed_real,
                    ],
                    axis=1,
                )
            )
            products.append(
                jnp.concatenate(
                    [
                        taps_real * gated_real + taps_imag * gated_imag,
                        taps_real * gated_imag - taps_imag * gated_real,
                    ],
                    axis=1,
                )
            )
            lag_real = lag_real + (mixed_real * gated_real + mixed_imag * gated_imag)
            lag_imag = lag_imag + (mixed_real * gated_imag - mixed_imag * gated_real)
        last = start + GROUP == SEQS
        if last:
            products.append(jnp.concatenate([lag_real, lag_imag], axis=1))
        rows = inner(products, inner_back_ref)
        for index in range(GROUP):
            result = outer_back(rows[2 * index * HALF : 2 * (index + 1) * HALF])
            base = (start + index) * OWNERS * ROWS_OUT
            store(result[:, :LANES], base)
            store(result[:, LANES:], base + PIECES)
        if last:
            lag = outer_back(rows[2 * GROUP * HALF :])
    for seq in range(SEQS):
        store(lag, seq * OWNERS * ROWS_OUT + 2 * PIECES)


def post_kernel(c_ref, q_ref, k_ref, v_ref, u_ref, o_ref, qg_ref, kg_ref, vg_ref, fg_ref):
    for piece in range(PIECES):
        at = pl.ds(piece * LANES, LANES)
        conv = c_ref[pl.ds(piece, CHANNELS, stride=ROWS_OUT), :].T
        back = c_ref[pl.ds(PIECES + piece, CHANNELS, stride=ROWS_OUT), :].T
        o_ref[0, at, :] = (q_ref[0, at, :].astype(jnp.float32) * conv).astype(jnp.bfloat16)
        qg_ref[0, at, :] = (u_ref[0, at, :].astype(jnp.float32) * conv).astype(jnp.bfloat16)
        kg_ref[0, at, :] = (back * v_ref[0, at, :].astype(jnp.float32)).astype(jnp.bfloat16)
        vg_ref[0, at, :] = (back * k_ref[0, at, :].astype(jnp.float32)).astype(jnp.bfloat16)
        fg_ref[at, :] = c_ref[pl.ds(2 * PIECES + piece, CHANNELS, stride=ROWS_OUT), :].T


def params():
    return pltpu.CompilerParams(vmem_limit_bytes=VMEM_LIMIT)


def pre(part, query_seq, key_seq, value_seq, upstream, filter_param):
    whole = pl.BlockSpec((1, BLOCK, CHANNELS), lambda i, part: (0, 0, 0))
    return pl.pallas_call(
        pre_kernel,
        out_shape=jax.ShapeDtypeStruct((CHANNELS * ROWS_IN, LANES), jnp.float32),
        grid_spec=pltpu.PrefetchScalarGridSpec(
            num_scalar_prefetch=1,
            grid=(1,),
            in_specs=[whole] * 4 + [pl.BlockSpec((LANES, CHANNELS), lambda i, part: (part[0], 0))],
            out_specs=pl.BlockSpec((CHANNELS * ROWS_IN, LANES), lambda i, part: (0, 0)),
        ),
        compiler_params=params(),
    )(part, query_seq, key_seq, value_seq, upstream, filter_param)


def transform(arrived, tables):
    return pl.pallas_call(
        fft_kernel,
        out_shape=jax.ShapeDtypeStruct((SEQS * OWNERS * ROWS_OUT, LANES), jnp.float32),
        compiler_params=params(),
    )(arrived, *tables)


def post(returned, query_seq, key_seq, value_seq, upstream):
    half = jax.ShapeDtypeStruct((1, BLOCK, CHANNELS), jnp.bfloat16)
    return pl.pallas_call(
        post_kernel,
        out_shape=(half, half, half, half, jax.ShapeDtypeStruct((BLOCK, CHANNELS), jnp.float32)),
        compiler_params=params(),
    )(returned, query_seq, key_seq, value_seq, upstream)


def exchange(rows, depth):
    shaped = rows.reshape(CHANNELS, depth, 1, LANES)
    moved = lax.all_to_all(shaped, ("dp", "seq"), split_axis=0, concat_axis=0, tiled=True)
    return moved.reshape(CHANNELS * depth, LANES)


def local(query_seq, key_seq, value_seq, upstream, filter_param):
    tables = [jnp.asarray(table) for table in constants()]
    part = lax.div(lax.axis_index("dp"), 2).astype(jnp.int32).reshape(1)
    sent = pre(part, query_seq, key_seq, value_seq, upstream, filter_param)
    arrived = exchange(sent, ROWS_IN)
    results = transform(arrived, tables)
    returned = exchange(results, ROWS_OUT)
    return post(returned, query_seq, key_seq, value_seq, upstream)


def solution(mesh):
    in_specs = (
        P("dp", "seq", None),
        P("dp", "seq", None),
        P("dp", "seq", None),
        P("dp", "seq", None),
        P("seq", None),
    )
    out_specs = (
        P("dp", "seq", None),
        P("dp", "seq", None),
        P("dp", "seq", None),
        P("dp", "seq", None),
        P("seq", None),
    )
    return jax.shard_map(local, mesh=mesh, in_specs=in_specs, out_specs=out_specs, check_vma=False)
```

```python
import math

import jax
import jax.numpy as jnp
import ml_dtypes
import numpy as np
from jax import lax
from jax.experimental import pallas as pl
from jax.experimental.pallas import tpu as pltpu
from jax.sharding import PartitionSpec as P

LANES = 128
BLOCK = 512
CHANNELS = 256
SEQS = 8
OWNERS = 32
PIECES = BLOCK // LANES
ROWS_IN = 2 * PIECES + 1
ROWS_OUT = 3 * PIECES
HALF = 128
LENGTH = 2 * BLOCK * OWNERS
GROUP = 4
VMEM_LIMIT = 32 << 20
PRE_VMEM_LIMIT = 56 << 20


def split_parts(values):
    high = values.astype(np.float32).astype(ml_dtypes.bfloat16)
    low = (values - high.astype(np.float64)).astype(np.float32).astype(ml_dtypes.bfloat16)
    return high, low


def constants():
    freq = np.arange(HALF, dtype=np.int64)
    rows = np.arange(HALF, dtype=np.int64)
    coarse = (rows % OWNERS) * PIECES + rows // OWNERS
    turn = 2.0 * np.pi * (np.outer(2 * freq + 1, coarse) % (4 * HALF)) / (4 * HALF)
    outer = np.concatenate([np.cos(turn), -np.sin(turn)], axis=0)
    outer_high, outer_low = split_parts(outer)
    outer_cat = np.concatenate([outer_high, outer_high, outer_low], axis=1)
    scale = 2.0 / LENGTH / math.sqrt(LENGTH // 2)
    back_outer = outer.T * scale
    back_high, back_low = split_parts(back_outer)
    back_cat = np.concatenate([back_high, back_high, back_low], axis=1)
    lanes = np.arange(LANES, dtype=np.int64)
    inner_turn = 2.0 * np.pi * (np.outer(lanes, lanes) % LANES) / LANES
    cos_in, sin_in = np.cos(inner_turn), np.sin(inner_turn)
    inner = np.block([[cos_in, -sin_in], [sin_in, cos_in]])
    inner_high, inner_low = split_parts(inner)
    inner_cat = np.concatenate([inner_high, inner_high, inner_low], axis=0)
    inner_back = np.concatenate([inner_high.T, inner_high.T, inner_low.T], axis=0)
    twist = 2.0 * np.pi * np.outer(2 * freq + 1, lanes) / (2 * LENGTH)
    twiddle = np.stack([np.cos(twist), np.sin(twist)]).astype(np.float32)
    return (outer_cat, inner_cat, inner_back, back_cat, twiddle)


def pre_kernel(part_ref, q_hbm, k_hbm, v_hbm, u_hbm, f_hbm, out_ref, data, taps, sems, taps_sem):
    sources = (k_hbm, v_hbm, u_hbm, q_hbm)
    copies = []
    for piece in range(PIECES):
        at = pl.ds(piece * LANES, LANES)
        copies.append(
            [
                pltpu.make_async_copy(source.at[0, at, :], data.at[index, at, :], sems.at[index, piece])
                for index, source in enumerate(sources)
            ]
        )
        for copy in copies[-1]:
            copy.start()
    first = pl.multiple_of(part_ref[0] * LANES, LANES)
    taps_copy = pltpu.make_async_copy(f_hbm.at[pl.ds(first, LANES), :], taps, taps_sem)
    taps_copy.start()
    for piece in range(PIECES):
        for copy in copies[piece]:
            copy.wait()
        key, value, grad, query = [
            data[index, pl.ds(piece * LANES, LANES), :].astype(jnp.float32) for index in range(4)
        ]
        out_ref[pl.ds(piece, CHANNELS, stride=ROWS_IN), :] = (key * value).T
        out_ref[pl.ds(PIECES + piece, CHANNELS, stride=ROWS_IN), :] = (grad * query).T
    taps_copy.wait()
    out_ref[pl.ds(2 * PIECES, CHANNELS, stride=ROWS_IN), :] = taps[...].T


def halves(value, axis):
    high = value.astype(jnp.bfloat16)
    low = (value - high.astype(jnp.float32)).astype(jnp.bfloat16)
    return jnp.concatenate([high, low, high], axis=axis)


def dot(left, right):
    return jnp.dot(left, right, preferred_element_type=jnp.float32)


def fft_kernel(in_ref, outer_ref, inner_ref, inner_back_ref, back_ref, twiddle_ref, out_ref):
    cos_t = twiddle_ref[0]
    sin_t = twiddle_ref[1]

    def load(base):
        return jnp.concatenate(
            [in_ref[pl.ds(base + piece, OWNERS, stride=ROWS_IN), :] for piece in range(PIECES)], axis=0
        )

    def outer(signals):
        first = dot(outer_ref[...], halves(jnp.concatenate(signals, axis=1), 0))
        turned = []
        for index in range(len(signals)):
            at = slice(index * LANES, (index + 1) * LANES)
            real, imag = first[:HALF, at], first[HALF:, at]
            turned.append(
                jnp.concatenate([real * cos_t + imag * sin_t, imag * cos_t - real * sin_t], axis=1)
            )
        return turned

    def inner(blocks, table_ref):
        return dot(halves(jnp.concatenate(blocks, axis=0), 1), table_ref[...])

    def outer_back(rows):
        turned = []
        for index in range(rows.shape[0] // HALF):
            at = slice(index * HALF, (index + 1) * HALF)
            real, imag = rows[at, :LANES], rows[at, LANES:]
            turned.append(
                jnp.concatenate([real * cos_t - imag * sin_t, imag * cos_t + real * sin_t], axis=0)
            )
        return dot(back_ref[...], halves(jnp.concatenate(turned, axis=1), 0))

    def store(result, base):
        for piece in range(PIECES):
            out_ref[pl.ds(base + piece, OWNERS, stride=ROWS_OUT), :] = result[
                piece * OWNERS : (piece + 1) * OWNERS, :
            ]

    taps = jnp.concatenate(
        [
            in_ref[pl.ds(2 * piece * OWNERS * ROWS_IN + 2 * PIECES, OWNERS, stride=ROWS_IN), :]
            for piece in range(PIECES)
        ],
        axis=0,
    )
    lag_real = jnp.zeros((HALF, LANES), jnp.float32)
    lag_imag = jnp.zeros((HALF, LANES), jnp.float32)
    for start in range(0, SEQS, GROUP):
        turned = []
        for seq in range(start, start + GROUP):
            base = seq * OWNERS * ROWS_IN
            turned += outer([load(base), load(base + PIECES)])
        if start == 0:
            turned += outer([taps])
        spec = inner(turned, inner_ref)
        if start == 0:
            taps_real, taps_imag = spec[2 * GROUP * HALF :, :LANES], spec[2 * GROUP * HALF :, LANES:]
        products = []
        for index in range(GROUP):
            at = slice(2 * index * HALF, (2 * index + 1) * HALF)
            mixed_real, mixed_imag = spec[at, :LANES], spec[at, LANES:]
            at = slice((2 * index + 1) * HALF, (2 * index + 2) * HALF)
            gated_real, gated_imag = spec[at, :LANES], spec[at, LANES:]
            products.append(
                jnp.concatenate(
                    [
                        taps_real * mixed_real - taps_imag * mixed_imag,
                        taps_real * mixed_imag + taps_imag * mixed_real,
                    ],
                    axis=1,
                )
            )
            products.append(
                jnp.concatenate(
                    [
                        taps_real * gated_real + taps_imag * gated_imag,
                        taps_real * gated_imag - taps_imag * gated_real,
                    ],
                    axis=1,
                )
            )
            lag_real = lag_real + (mixed_real * gated_real + mixed_imag * gated_imag)
            lag_imag = lag_imag + (mixed_real * gated_imag - mixed_imag * gated_real)
        last = start + GROUP == SEQS
        if last:
            products.append(jnp.concatenate([lag_real, lag_imag], axis=1))
        rows = inner(products, inner_back_ref)
        for index in range(GROUP):
            result = outer_back(rows[2 * index * HALF : 2 * (index + 1) * HALF])
            base = (start + index) * OWNERS * ROWS_OUT
            store(result[:, :LANES], base)
            store(result[:, LANES:], base + PIECES)
        if last:
            lag = outer_back(rows[2 * GROUP * HALF :])
    for seq in range(SEQS):
        store(lag, seq * OWNERS * ROWS_OUT + 2 * PIECES)


def post_kernel(
    c_ref, q_ref, k_ref, v_ref, u_ref, o_hbm, qg_hbm, kg_hbm, vg_hbm, fg_hbm, small, large, sems, large_sems
):
    copies = []
    for piece in range(PIECES):
        at = pl.ds(piece * LANES, LANES)
        conv = c_ref[pl.ds(piece, CHANNELS, stride=ROWS_OUT), :].T
        back = c_ref[pl.ds(PIECES + piece, CHANNELS, stride=ROWS_OUT), :].T
        large[at, :] = c_ref[pl.ds(2 * PIECES + piece, CHANNELS, stride=ROWS_OUT), :].T
        pieces = (
            (q_ref, conv, o_hbm),
            (u_ref, conv, qg_hbm),
            (v_ref, back, kg_hbm),
            (k_ref, back, vg_hbm),
        )
        for index, (factor, result, target) in enumerate(pieces):
            small[index, at, :] = (factor[0, at, :].astype(jnp.float32) * result).astype(jnp.bfloat16)
            copies.append(
                pltpu.make_async_copy(small.at[index, at, :], target.at[0, at, :], sems.at[index, piece])
            )
            copies[-1].start()
        copies.append(pltpu.make_async_copy(large.at[at, :], fg_hbm.at[at, :], large_sems.at[piece]))
        copies[-1].start()
    for copy in copies:
        copy.wait()


def params(limit=VMEM_LIMIT):
    return pltpu.CompilerParams(vmem_limit_bytes=limit)


def pre(part, query_seq, key_seq, value_seq, upstream, filter_param):
    return pl.pallas_call(
        pre_kernel,
        out_shape=jax.ShapeDtypeStruct((CHANNELS * ROWS_IN, LANES), jnp.float32),
        in_specs=[pl.BlockSpec(memory_space=pltpu.SMEM)] + [pl.BlockSpec(memory_space=pltpu.HBM)] * 5,
        out_specs=pl.BlockSpec(memory_space=pltpu.VMEM),
        scratch_shapes=[
            pltpu.VMEM((4, BLOCK, CHANNELS), jnp.bfloat16),
            pltpu.VMEM((LANES, CHANNELS), jnp.float32),
            pltpu.SemaphoreType.DMA((4, PIECES)),
            pltpu.SemaphoreType.DMA,
        ],
        compiler_params=params(PRE_VMEM_LIMIT),
    )(part, query_seq, key_seq, value_seq, upstream, filter_param)


def transform(arrived, tables):
    return pl.pallas_call(
        fft_kernel,
        out_shape=jax.ShapeDtypeStruct((SEQS * OWNERS * ROWS_OUT, LANES), jnp.float32),
        compiler_params=params(),
    )(arrived, *tables)


def post(returned, query_seq, key_seq, value_seq, upstream):
    half = jax.ShapeDtypeStruct((1, BLOCK, CHANNELS), jnp.bfloat16)
    return pl.pallas_call(
        post_kernel,
        out_shape=(half, half, half, half, jax.ShapeDtypeStruct((BLOCK, CHANNELS), jnp.float32)),
        in_specs=[pl.BlockSpec(memory_space=pltpu.VMEM)] * 5,
        out_specs=[pl.BlockSpec(memory_space=pltpu.HBM)] * 5,
        scratch_shapes=[
            pltpu.VMEM((4, BLOCK, CHANNELS), jnp.bfloat16),
            pltpu.VMEM((BLOCK, CHANNELS), jnp.float32),
            pltpu.SemaphoreType.DMA((4, PIECES)),
            pltpu.SemaphoreType.DMA((PIECES,)),
        ],
        compiler_params=params(),
    )(returned, query_seq, key_seq, value_seq, upstream)


def exchange(rows, depth):
    shaped = rows.reshape(CHANNELS, depth, 1, LANES)
    moved = lax.all_to_all(shaped, ("dp", "seq"), split_axis=0, concat_axis=0, tiled=True)
    return moved.reshape(CHANNELS * depth, LANES)


def local(query_seq, key_seq, value_seq, upstream, filter_param):
    tables = [jnp.asarray(table) for table in constants()]
    part = lax.div(lax.axis_index("dp"), 2).astype(jnp.int32).reshape(1)
    sent = pre(part, query_seq, key_seq, value_seq, upstream, filter_param)
    arrived = exchange(sent, ROWS_IN)
    results = transform(arrived, tables)
    returned = exchange(results, ROWS_OUT)
    return post(returned, query_seq, key_seq, value_seq, upstream)


def solution(mesh):
    in_specs = (
        P("dp", "seq", None),
        P("dp", "seq", None),
        P("dp", "seq", None),
        P("dp", "seq", None),
        P("seq", None),
    )
    out_specs = (
        P("dp", "seq", None),
        P("dp", "seq", None),
        P("dp", "seq", None),
        P("dp", "seq", None),
        P("seq", None),
    )
    return jax.shard_map(local, mesh=mesh, in_specs=in_specs, out_specs=out_specs, check_vma=False)
```

```python
import math

import jax
import jax.numpy as jnp
import ml_dtypes
import numpy as np
from jax import lax
from jax.experimental import pallas as pl
from jax.experimental.pallas import tpu as pltpu
from jax.sharding import PartitionSpec as P

LANES = 128
BLOCK = 512
CHANNELS = 256
SEQS = 8
OWNERS = 32
PIECES = BLOCK // LANES
ROWS_IN = 2 * PIECES + 1
ROWS_OUT = 3 * PIECES
HALF = 128
LENGTH = 2 * BLOCK * OWNERS
GROUP = 4
VMEM_LIMIT = 32 << 20


def split_parts(values):
    high = values.astype(np.float32).astype(ml_dtypes.bfloat16)
    low = (values - high.astype(np.float64)).astype(np.float32).astype(ml_dtypes.bfloat16)
    return high, low


def constants():
    freq = np.arange(HALF, dtype=np.int64)
    rows = np.arange(HALF, dtype=np.int64)
    coarse = (rows % OWNERS) * PIECES + rows // OWNERS
    turn = 2.0 * np.pi * (np.outer(2 * freq + 1, coarse) % (4 * HALF)) / (4 * HALF)
    outer = np.concatenate([np.cos(turn), -np.sin(turn)], axis=0)
    outer_high, outer_low = split_parts(outer)
    outer_cat = np.concatenate([outer_high, outer_high, outer_low], axis=1)
    scale = 2.0 / LENGTH / math.sqrt(LENGTH // 2)
    back_outer = outer.T * scale
    back_high, back_low = split_parts(back_outer)
    back_cat = np.concatenate([back_high, back_high, back_low], axis=1)
    lanes = np.arange(LANES, dtype=np.int64)
    inner_turn = 2.0 * np.pi * (np.outer(lanes, lanes) % LANES) / LANES
    cos_in, sin_in = np.cos(inner_turn), np.sin(inner_turn)
    inner = np.block([[cos_in, -sin_in], [sin_in, cos_in]])
    inner_high, inner_low = split_parts(inner)
    inner_cat = np.concatenate([inner_high, inner_high, inner_low], axis=0)
    inner_back = np.concatenate([inner_high.T, inner_high.T, inner_low.T], axis=0)
    twist = 2.0 * np.pi * np.outer(2 * freq + 1, lanes) / (2 * LENGTH)
    twiddle = np.stack([np.cos(twist), np.sin(twist)]).astype(np.float32)
    return (outer_cat, inner_cat, inner_back, back_cat, twiddle)


def pre_kernel(part_ref, q_hbm, k_hbm, v_hbm, u_hbm, f_hbm, out_ref, data, taps, sems, taps_sem):
    sources = (k_hbm, v_hbm, u_hbm, q_hbm)
    copies = []
    for piece in range(PIECES):
        at = pl.ds(piece * LANES, LANES)
        copies.append(
            [
                pltpu.make_async_copy(source.at[0, at, :], data.at[index, at, :], sems.at[index, piece])
                for index, source in enumerate(sources)
            ]
        )
        for copy in copies[-1]:
            copy.start()
    first = pl.multiple_of(part_ref[0] * LANES, LANES)
    taps_copy = pltpu.make_async_copy(f_hbm.at[pl.ds(first, LANES), :], taps, taps_sem)
    taps_copy.start()
    for piece in range(PIECES):
        for copy in copies[piece]:
            copy.wait()
        key, value, grad, query = [
            data[index, pl.ds(piece * LANES, LANES), :].astype(jnp.float32) for index in range(4)
        ]
        out_ref[pl.ds(piece, CHANNELS, stride=ROWS_IN), :] = (key * value).T
        out_ref[pl.ds(PIECES + piece, CHANNELS, stride=ROWS_IN), :] = (grad * query).T
    taps_copy.wait()
    out_ref[pl.ds(2 * PIECES, CHANNELS, stride=ROWS_IN), :] = taps[...].T


def halves(value, axis):
    high = value.astype(jnp.bfloat16)
    low = (value - high.astype(jnp.float32)).astype(jnp.bfloat16)
    return jnp.concatenate([high, low, high], axis=axis)


def dot(left, right):
    return jnp.dot(left, right, preferred_element_type=jnp.float32)


def fft_kernel(in_ref, outer_ref, inner_ref, inner_back_ref, back_ref, twiddle_ref, out_ref):
    cos_t = twiddle_ref[0]
    sin_t = twiddle_ref[1]

    def load(base):
        return jnp.concatenate(
            [in_ref[pl.ds(base + piece, OWNERS, stride=ROWS_IN), :] for piece in range(PIECES)], axis=0
        )

    def outer(signals):
        first = dot(outer_ref[...], halves(jnp.concatenate(signals, axis=1), 0))
        turned = []
        for index in range(len(signals)):
            at = slice(index * LANES, (index + 1) * LANES)
            real, imag = first[:HALF, at], first[HALF:, at]
            turned.append(
                jnp.concatenate([real * cos_t + imag * sin_t, imag * cos_t - real * sin_t], axis=1)
            )
        return turned

    def inner(blocks, table_ref):
        return dot(halves(jnp.concatenate(blocks, axis=0), 1), table_ref[...])

    def outer_back(rows):
        turned = []
        for index in range(rows.shape[0] // HALF):
            at = slice(index * HALF, (index + 1) * HALF)
            real, imag = rows[at, :LANES], rows[at, LANES:]
            turned.append(
                jnp.concatenate([real * cos_t - imag * sin_t, imag * cos_t + real * sin_t], axis=0)
            )
        return dot(back_ref[...], halves(jnp.concatenate(turned, axis=1), 0))

    def store(result, base):
        for piece in range(PIECES):
            out_ref[pl.ds(base + piece, OWNERS, stride=ROWS_OUT), :] = result[
                piece * OWNERS : (piece + 1) * OWNERS, :
            ]

    taps = jnp.concatenate(
        [
            in_ref[pl.ds(2 * piece * OWNERS * ROWS_IN + 2 * PIECES, OWNERS, stride=ROWS_IN), :]
            for piece in range(PIECES)
        ],
        axis=0,
    )
    lag_real = jnp.zeros((HALF, LANES), jnp.float32)
    lag_imag = jnp.zeros((HALF, LANES), jnp.float32)
    for start in range(0, SEQS, GROUP):
        turned = []
        for seq in range(start, start + GROUP):
            base = seq * OWNERS * ROWS_IN
            turned += outer([load(base), load(base + PIECES)])
        if start == 0:
            turned += outer([taps])
        spec = inner(turned, inner_ref)
        if start == 0:
            taps_real, taps_imag = spec[2 * GROUP * HALF :, :LANES], spec[2 * GROUP * HALF :, LANES:]
        products = []
        for index in range(GROUP):
            at = slice(2 * index * HALF, (2 * index + 1) * HALF)
            mixed_real, mixed_imag = spec[at, :LANES], spec[at, LANES:]
            at = slice((2 * index + 1) * HALF, (2 * index + 2) * HALF)
            gated_real, gated_imag = spec[at, :LANES], spec[at, LANES:]
            products.append(
                jnp.concatenate(
                    [
                        taps_real * mixed_real - taps_imag * mixed_imag,
                        taps_real * mixed_imag + taps_imag * mixed_real,
                    ],
                    axis=1,
                )
            )
            products.append(
                jnp.concatenate(
                    [
                        taps_real * gated_real + taps_imag * gated_imag,
                        taps_real * gated_imag - taps_imag * gated_real,
                    ],
                    axis=1,
                )
            )
            lag_real = lag_real + (mixed_real * gated_real + mixed_imag * gated_imag)
            lag_imag = lag_imag + (mixed_real * gated_imag - mixed_imag * gated_real)
        last = start + GROUP == SEQS
        if last:
            products.append(jnp.concatenate([lag_real, lag_imag], axis=1))
        rows = inner(products, inner_back_ref)
        for index in range(GROUP):
            result = outer_back(rows[2 * index * HALF : 2 * (index + 1) * HALF])
            base = (start + index) * OWNERS * ROWS_OUT
            store(result[:, :LANES], base)
            store(result[:, LANES:], base + PIECES)
        if last:
            lag = outer_back(rows[2 * GROUP * HALF :])
    for seq in range(SEQS):
        store(lag, seq * OWNERS * ROWS_OUT + 2 * PIECES)


def post_kernel(
    c_ref, q_ref, k_ref, v_ref, u_ref, o_hbm, qg_hbm, kg_hbm, vg_hbm, fg_hbm, small, large, sems, large_sems
):
    copies = []
    for piece in range(PIECES):
        at = pl.ds(piece * LANES, LANES)
        conv = c_ref[pl.ds(piece, CHANNELS, stride=ROWS_OUT), :].T
        back = c_ref[pl.ds(PIECES + piece, CHANNELS, stride=ROWS_OUT), :].T
        large[at, :] = c_ref[pl.ds(2 * PIECES + piece, CHANNELS, stride=ROWS_OUT), :].T
        pieces = (
            (q_ref, conv, o_hbm),
            (u_ref, conv, qg_hbm),
            (v_ref, back, kg_hbm),
            (k_ref, back, vg_hbm),
        )
        for index, (factor, result, target) in enumerate(pieces):
            small[index, at, :] = (factor[0, at, :].astype(jnp.float32) * result).astype(jnp.bfloat16)
            copies.append(
                pltpu.make_async_copy(small.at[index, at, :], target.at[0, at, :], sems.at[index, piece])
            )
            copies[-1].start()
        copies.append(pltpu.make_async_copy(large.at[at, :], fg_hbm.at[at, :], large_sems.at[piece]))
        copies[-1].start()
    for copy in copies:
        copy.wait()


def params():
    return pltpu.CompilerParams(vmem_limit_bytes=VMEM_LIMIT)


def pre(part, *arrays):
    arrays = [pltpu.with_memory_space_constraint(array, pltpu.HBM) for array in arrays]
    return pl.pallas_call(
        pre_kernel,
        out_shape=jax.ShapeDtypeStruct((CHANNELS * ROWS_IN, LANES), jnp.float32),
        in_specs=[pl.BlockSpec(memory_space=pltpu.SMEM)] + [pl.BlockSpec(memory_space=pltpu.HBM)] * 5,
        out_specs=pl.BlockSpec(memory_space=pltpu.VMEM),
        scratch_shapes=[
            pltpu.VMEM((4, BLOCK, CHANNELS), jnp.bfloat16),
            pltpu.VMEM((LANES, CHANNELS), jnp.float32),
            pltpu.SemaphoreType.DMA((4, PIECES)),
            pltpu.SemaphoreType.DMA,
        ],
        compiler_params=params(),
    )(part, *arrays)


def transform(arrived, tables):
    return pl.pallas_call(
        fft_kernel,
        out_shape=jax.ShapeDtypeStruct((SEQS * OWNERS * ROWS_OUT, LANES), jnp.float32),
        compiler_params=params(),
    )(arrived, *tables)


def post(returned, query_seq, key_seq, value_seq, upstream):
    half = jax.ShapeDtypeStruct((1, BLOCK, CHANNELS), jnp.bfloat16)
    return pl.pallas_call(
        post_kernel,
        out_shape=(half, half, half, half, jax.ShapeDtypeStruct((BLOCK, CHANNELS), jnp.float32)),
        in_specs=[pl.BlockSpec(memory_space=pltpu.VMEM)] * 5,
        out_specs=[pl.BlockSpec(memory_space=pltpu.HBM)] * 5,
        scratch_shapes=[
            pltpu.VMEM((4, BLOCK, CHANNELS), jnp.bfloat16),
            pltpu.VMEM((BLOCK, CHANNELS), jnp.float32),
            pltpu.SemaphoreType.DMA((4, PIECES)),
            pltpu.SemaphoreType.DMA((PIECES,)),
        ],
        compiler_params=params(),
    )(returned, query_seq, key_seq, value_seq, upstream)


def exchange(rows, depth):
    shaped = rows.reshape(CHANNELS, depth, 1, LANES)
    moved = lax.all_to_all(shaped, ("dp", "seq"), split_axis=0, concat_axis=0, tiled=True)
    return moved.reshape(CHANNELS * depth, LANES)


def local(query_seq, key_seq, value_seq, upstream, filter_param):
    tables = [jnp.asarray(table) for table in constants()]
    part = lax.div(lax.axis_index("dp"), 2).astype(jnp.int32).reshape(1)
    sent = pre(part, query_seq, key_seq, value_seq, upstream, filter_param)
    arrived = exchange(sent, ROWS_IN)
    results = transform(arrived, tables)
    returned = exchange(results, ROWS_OUT)
    return post(returned, query_seq, key_seq, value_seq, upstream)


def solution(mesh):
    in_specs = (
        P("dp", "seq", None),
        P("dp", "seq", None),
        P("dp", "seq", None),
        P("dp", "seq", None),
        P("seq", None),
    )
    out_specs = (
        P("dp", "seq", None),
        P("dp", "seq", None),
        P("dp", "seq", None),
        P("dp", "seq", None),
        P("seq", None),
    )
    return jax.shard_map(local, mesh=mesh, in_specs=in_specs, out_specs=out_specs, check_vma=False)
```

```python
import math

import jax
import jax.numpy as jnp
import ml_dtypes
import numpy as np
from jax import lax
from jax.experimental import pallas as pl
from jax.experimental.pallas import tpu as pltpu
from jax.sharding import PartitionSpec as P

LANES = 128
BLOCK = 512
CHANNELS = 256
SEQS = 8
OWNERS = 32
PIECES = BLOCK // LANES
ROWS_IN = 2 * PIECES + 1
ROWS_OUT = 2 * PIECES
Z_CHIPS = 8
HALF = 128
LENGTH = 2 * BLOCK * OWNERS
GROUP = 4
VMEM_LIMIT = 32 << 20


def split_parts(values):
    high = values.astype(np.float32).astype(ml_dtypes.bfloat16)
    low = (values - high.astype(np.float64)).astype(np.float32).astype(ml_dtypes.bfloat16)
    return high, low


def constants():
    freq = np.arange(HALF, dtype=np.int64)
    rows = np.arange(HALF, dtype=np.int64)
    coarse = (rows % OWNERS) * PIECES + rows // OWNERS
    turn = 2.0 * np.pi * (np.outer(2 * freq + 1, coarse) % (4 * HALF)) / (4 * HALF)
    outer = np.concatenate([np.cos(turn), -np.sin(turn)], axis=0)
    outer_high, outer_low = split_parts(outer)
    outer_cat = np.concatenate([outer_high, outer_high, outer_low], axis=1)
    scale = 2.0 / LENGTH / math.sqrt(LENGTH // 2)
    back_outer = outer.T * scale
    back_high, back_low = split_parts(back_outer)
    back_cat = np.concatenate([back_high, back_high, back_low], axis=1)
    lanes = np.arange(LANES, dtype=np.int64)
    inner_turn = 2.0 * np.pi * (np.outer(lanes, lanes) % LANES) / LANES
    cos_in, sin_in = np.cos(inner_turn), np.sin(inner_turn)
    inner = np.block([[cos_in, -sin_in], [sin_in, cos_in]])
    inner_high, inner_low = split_parts(inner)
    inner_cat = np.concatenate([inner_high, inner_high, inner_low], axis=0)
    inner_back = np.concatenate([inner_high.T, inner_high.T, inner_low.T], axis=0)
    twist = 2.0 * np.pi * np.outer(2 * freq + 1, lanes) / (2 * LENGTH)
    twiddle = np.stack([np.cos(twist), np.sin(twist)]).astype(np.float32)
    return (outer_cat, inner_cat, inner_back, back_cat, twiddle)


def pre_kernel(part_ref, q_hbm, k_hbm, v_hbm, u_hbm, f_hbm, out_ref, data, taps, sems, taps_sem):
    sources = (k_hbm, v_hbm, u_hbm, q_hbm)
    copies = []
    for piece in range(PIECES):
        at = pl.ds(piece * LANES, LANES)
        copies.append(
            [
                pltpu.make_async_copy(source.at[0, at, :], data.at[index, at, :], sems.at[index, piece])
                for index, source in enumerate(sources)
            ]
        )
        for copy in copies[-1]:
            copy.start()
    first = pl.multiple_of(part_ref[0] * LANES, LANES)
    taps_copy = pltpu.make_async_copy(f_hbm.at[pl.ds(first, LANES), :], taps, taps_sem)
    taps_copy.start()
    for piece in range(PIECES):
        for copy in copies[piece]:
            copy.wait()
        key, value, grad, query = [
            data[index, pl.ds(piece * LANES, LANES), :].astype(jnp.float32) for index in range(4)
        ]
        out_ref[pl.ds(piece, CHANNELS, stride=ROWS_IN), :] = (key * value).T
        out_ref[pl.ds(PIECES + piece, CHANNELS, stride=ROWS_IN), :] = (grad * query).T
    taps_copy.wait()
    out_ref[pl.ds(2 * PIECES, CHANNELS, stride=ROWS_IN), :] = taps[...].T


def halves(value, axis):
    high = value.astype(jnp.bfloat16)
    low = (value - high.astype(jnp.float32)).astype(jnp.bfloat16)
    return jnp.concatenate([high, low, high], axis=axis)


def dot(left, right):
    return jnp.dot(left, right, preferred_element_type=jnp.float32)


def fft_kernel(
    place_ref, in_ref, outer_ref, inner_ref, inner_back_ref, back_ref, twiddle_ref, out_ref, lag_ref, blocks
):
    cos_t = twiddle_ref[0]
    sin_t = twiddle_ref[1]

    def load(base):
        return jnp.concatenate(
            [in_ref[pl.ds(base + piece, OWNERS, stride=ROWS_IN), :] for piece in range(PIECES)], axis=0
        )

    def outer(signals):
        first = dot(outer_ref[...], halves(jnp.concatenate(signals, axis=1), 0))
        turned = []
        for index in range(len(signals)):
            at = slice(index * LANES, (index + 1) * LANES)
            real, imag = first[:HALF, at], first[HALF:, at]
            turned.append(
                jnp.concatenate([real * cos_t + imag * sin_t, imag * cos_t - real * sin_t], axis=1)
            )
        return turned

    def inner(blocks, table_ref):
        return dot(halves(jnp.concatenate(blocks, axis=0), 1), table_ref[...])

    def outer_back(rows):
        turned = []
        for index in range(rows.shape[0] // HALF):
            at = slice(index * HALF, (index + 1) * HALF)
            real, imag = rows[at, :LANES], rows[at, LANES:]
            turned.append(
                jnp.concatenate([real * cos_t - imag * sin_t, imag * cos_t + real * sin_t], axis=0)
            )
        return dot(back_ref[...], halves(jnp.concatenate(turned, axis=1), 0))

    def store(result, base):
        for piece in range(PIECES):
            out_ref[pl.ds(base + piece, OWNERS, stride=ROWS_OUT), :] = result[
                piece * OWNERS : (piece + 1) * OWNERS, :
            ]

    taps = jnp.concatenate(
        [
            in_ref[pl.ds(2 * piece * OWNERS * ROWS_IN + 2 * PIECES, OWNERS, stride=ROWS_IN), :]
            for piece in range(PIECES)
        ],
        axis=0,
    )
    lag_real = jnp.zeros((HALF, LANES), jnp.float32)
    lag_imag = jnp.zeros((HALF, LANES), jnp.float32)
    for start in range(0, SEQS, GROUP):
        turned = []
        for seq in range(start, start + GROUP):
            base = seq * OWNERS * ROWS_IN
            turned += outer([load(base), load(base + PIECES)])
        if start == 0:
            turned += outer([taps])
        spec = inner(turned, inner_ref)
        if start == 0:
            taps_real, taps_imag = spec[2 * GROUP * HALF :, :LANES], spec[2 * GROUP * HALF :, LANES:]
        products = []
        for index in range(GROUP):
            at = slice(2 * index * HALF, (2 * index + 1) * HALF)
            mixed_real, mixed_imag = spec[at, :LANES], spec[at, LANES:]
            at = slice((2 * index + 1) * HALF, (2 * index + 2) * HALF)
            gated_real, gated_imag = spec[at, :LANES], spec[at, LANES:]
            products.append(
                jnp.concatenate(
                    [
                        taps_real * mixed_real - taps_imag * mixed_imag,
                        taps_real * mixed_imag + taps_imag * mixed_real,
                    ],
                    axis=1,
                )
            )
            products.append(
                jnp.concatenate(
                    [
                        taps_real * gated_real + taps_imag * gated_imag,
                        taps_real * gated_imag - taps_imag * gated_real,
                    ],
                    axis=1,
                )
            )
            lag_real = lag_real + (mixed_real * gated_real + mixed_imag * gated_imag)
            lag_imag = lag_imag + (mixed_real * gated_imag - mixed_imag * gated_real)
        last = start + GROUP == SEQS
        if last:
            products.append(jnp.concatenate([lag_real, lag_imag], axis=1))
        rows = inner(products, inner_back_ref)
        for index in range(GROUP):
            result = outer_back(rows[2 * index * HALF : 2 * (index + 1) * HALF])
            base = (start + index) * OWNERS * ROWS_OUT
            store(result[:, :LANES], base)
            store(result[:, LANES:], base + PIECES)
        if last:
            lag = outer_back(rows[2 * GROUP * HALF :])
    for piece in range(PIECES):
        blocks[:, piece, :] = lag[piece * OWNERS : (piece + 1) * OWNERS, :]
    for other in range(OWNERS):
        lag_ref[other] = blocks[lax.bitwise_xor(place_ref[1], other)]


def post_kernel(c_ref, q_ref, k_ref, v_ref, u_ref, o_hbm, qg_hbm, kg_hbm, vg_hbm, small, sems):
    copies = []
    for piece in range(PIECES):
        at = pl.ds(piece * LANES, LANES)
        conv = c_ref[pl.ds(piece, CHANNELS, stride=ROWS_OUT), :].T
        back = c_ref[pl.ds(PIECES + piece, CHANNELS, stride=ROWS_OUT), :].T
        pieces = (
            (q_ref, conv, o_hbm),
            (u_ref, conv, qg_hbm),
            (v_ref, back, kg_hbm),
            (k_ref, back, vg_hbm),
        )
        for index, (factor, result, target) in enumerate(pieces):
            small[index, at, :] = (factor[0, at, :].astype(jnp.float32) * result).astype(jnp.bfloat16)
            copies.append(
                pltpu.make_async_copy(small.at[index, at, :], target.at[0, at, :], sems.at[index, piece])
            )
            copies[-1].start()
    for copy in copies:
        copy.wait()


def taps_kernel(place_ref, *refs):
    sources, fg_ref, blocks = refs[:SEQS], refs[SEQS], refs[SEQS + 1]
    for other, source in enumerate(sources):
        row = lax.bitwise_xor(place_ref[0], other) * OWNERS
        for index in range(OWNERS):
            blocks[row + lax.bitwise_xor(place_ref[1], index)] = source[index]
    for piece in range(PIECES):
        fg_ref[pl.ds(piece * LANES, LANES), :] = blocks[:, piece, :].T


def params():
    return pltpu.CompilerParams(vmem_limit_bytes=VMEM_LIMIT)


def pre(part, *arrays):
    arrays = [pltpu.with_memory_space_constraint(array, pltpu.HBM) for array in arrays]
    return pl.pallas_call(
        pre_kernel,
        out_shape=jax.ShapeDtypeStruct((CHANNELS * ROWS_IN, LANES), jnp.float32),
        in_specs=[pl.BlockSpec(memory_space=pltpu.SMEM)] + [pl.BlockSpec(memory_space=pltpu.HBM)] * 5,
        out_specs=pl.BlockSpec(memory_space=pltpu.VMEM),
        scratch_shapes=[
            pltpu.VMEM((4, BLOCK, CHANNELS), jnp.bfloat16),
            pltpu.VMEM((LANES, CHANNELS), jnp.float32),
            pltpu.SemaphoreType.DMA((4, PIECES)),
            pltpu.SemaphoreType.DMA,
        ],
        compiler_params=params(),
    )(part, *arrays)


def transform(place, arrived, tables):
    return pl.pallas_call(
        fft_kernel,
        out_shape=(
            jax.ShapeDtypeStruct((SEQS * OWNERS * ROWS_OUT, LANES), jnp.float32),
            jax.ShapeDtypeStruct((OWNERS, PIECES, LANES), jnp.float32),
        ),
        in_specs=[pl.BlockSpec(memory_space=pltpu.SMEM)] + [pl.BlockSpec(memory_space=pltpu.VMEM)] * 6,
        out_specs=[pl.BlockSpec(memory_space=pltpu.VMEM)] * 2,
        scratch_shapes=[pltpu.VMEM((OWNERS, PIECES, LANES), jnp.float32)],
        compiler_params=params(),
    )(place, arrived, *tables)


def post(returned, query_seq, key_seq, value_seq, upstream):
    half = jax.ShapeDtypeStruct((1, BLOCK, CHANNELS), jnp.bfloat16)
    return pl.pallas_call(
        post_kernel,
        out_shape=(half, half, half, half),
        in_specs=[pl.BlockSpec(memory_space=pltpu.VMEM)] * 5,
        out_specs=[pl.BlockSpec(memory_space=pltpu.HBM)] * 4,
        scratch_shapes=[
            pltpu.VMEM((4, BLOCK, CHANNELS), jnp.bfloat16),
            pltpu.SemaphoreType.DMA((4, PIECES)),
        ],
        compiler_params=params(),
    )(returned, query_seq, key_seq, value_seq, upstream)


def taps_grad(place, sources):
    return pl.pallas_call(
        taps_kernel,
        out_shape=jax.ShapeDtypeStruct((BLOCK, CHANNELS), jnp.float32),
        in_specs=[pl.BlockSpec(memory_space=pltpu.SMEM)] + [pl.BlockSpec(memory_space=pltpu.VMEM)] * SEQS,
        out_specs=pl.BlockSpec(memory_space=pltpu.VMEM),
        scratch_shapes=[pltpu.VMEM((CHANNELS, PIECES, LANES), jnp.float32)],
        compiler_params=params(),
    )(place, *sources)


def exchange(rows, depth):
    shaped = rows.reshape(CHANNELS, depth, 1, LANES)
    moved = lax.all_to_all(shaped, ("dp", "seq"), split_axis=0, concat_axis=0, tiled=True)
    return moved.reshape(CHANNELS * depth, LANES)


def swap(value, axis, bits):
    return lax.ppermute(value, axis, [(place, place ^ bits) for place in range(lax.axis_size(axis))])


def spread(lag):
    halves_x = lag.reshape(2, Z_CHIPS, 2, PIECES, LANES)
    columns = [halves_x[:, 0]] + [swap(halves_x[:, z], "seq", 2 * z) for z in range(1, Z_CHIPS)]
    by_z = jnp.stack(columns, axis=1)
    by_x = jnp.stack([by_z[0], swap(by_z[1], "seq", 2 * Z_CHIPS)])
    mine = jnp.stack([by_x[:, :, 0], swap(by_x[:, :, 1], "seq", 1)], axis=2)
    mine = mine.reshape(OWNERS, PIECES, LANES)
    return [mine] + [swap(mine, "dp", other) for other in range(1, SEQS)]


def local(query_seq, key_seq, value_seq, upstream, filter_param):
    tables = [jnp.asarray(table) for table in constants()]
    place = jnp.stack([lax.axis_index("dp"), lax.axis_index("seq")]).astype(jnp.int32)
    part = lax.div(lax.axis_index("dp"), 2).astype(jnp.int32).reshape(1)
    sent = pre(part, query_seq, key_seq, value_seq, upstream, filter_param)
    arrived = exchange(sent, ROWS_IN)
    results, lag = transform(place, arrived, tables)
    returned = exchange(results, ROWS_OUT)
    filter_grad = taps_grad(place, spread(lag))
    return (*post(returned, query_seq, key_seq, value_seq, upstream), filter_grad)


def solution(mesh):
    in_specs = (
        P("dp", "seq", None),
        P("dp", "seq", None),
        P("dp", "seq", None),
        P("dp", "seq", None),
        P("seq", None),
    )
    out_specs = (
        P("dp", "seq", None),
        P("dp", "seq", None),
        P("dp", "seq", None),
        P("dp", "seq", None),
        P("seq", None),
    )
    return jax.shard_map(local, mesh=mesh, in_specs=in_specs, out_specs=out_specs, check_vma=False)
```

```python
import math

import jax
import jax.numpy as jnp
import ml_dtypes
import numpy as np
from jax import lax
from jax.experimental import pallas as pl
from jax.experimental.pallas import tpu as pltpu
from jax.sharding import PartitionSpec as P

LANES = 128
BLOCK = 512
CHANNELS = 256
SEQS = 8
OWNERS = 32
PIECES = BLOCK // LANES
ROWS_IN = 2 * PIECES + 1
ROWS_OUT = 3 * PIECES
HALF = 128
LENGTH = 2 * BLOCK * OWNERS
GROUP = 2
VMEM_LIMIT = 32 << 20


def split_parts(values):
    high = values.astype(np.float32).astype(ml_dtypes.bfloat16)
    low = (values - high.astype(np.float64)).astype(np.float32).astype(ml_dtypes.bfloat16)
    return high, low


def constants():
    freq = np.arange(HALF, dtype=np.int64)
    rows = np.arange(HALF, dtype=np.int64)
    coarse = (rows % OWNERS) * PIECES + rows // OWNERS
    turn = 2.0 * np.pi * (np.outer(2 * freq + 1, coarse) % (4 * HALF)) / (4 * HALF)
    outer = np.concatenate([np.cos(turn), -np.sin(turn)], axis=0)
    outer_high, outer_low = split_parts(outer)
    outer_cat = np.concatenate([outer_high, outer_high, outer_low], axis=1)
    scale = 2.0 / LENGTH / math.sqrt(LENGTH // 2)
    back_outer = outer.T * scale
    back_high, back_low = split_parts(back_outer)
    back_cat = np.concatenate([back_high, back_high, back_low], axis=1)
    lanes = np.arange(LANES, dtype=np.int64)
    inner_turn = 2.0 * np.pi * (np.outer(lanes, lanes) % LANES) / LANES
    cos_in, sin_in = np.cos(inner_turn), np.sin(inner_turn)
    inner = np.block([[cos_in, -sin_in], [sin_in, cos_in]])
    inner_high, inner_low = split_parts(inner)
    inner_cat = np.concatenate([inner_high, inner_high, inner_low], axis=0)
    inner_back = np.concatenate([inner_high.T, inner_high.T, inner_low.T], axis=0)
    twist = 2.0 * np.pi * np.outer(2 * freq + 1, lanes) / (2 * LENGTH)
    twiddle = np.stack([np.cos(twist), np.sin(twist)]).astype(np.float32)
    return (outer_cat, inner_cat, inner_back, back_cat, twiddle)


def pre_kernel(part_ref, q_hbm, k_hbm, v_hbm, u_hbm, f_hbm, out_ref, data, taps, sems, taps_sem):
    sources = (k_hbm, v_hbm, u_hbm, q_hbm)
    copies = []
    for piece in range(PIECES):
        at = pl.ds(piece * LANES, LANES)
        copies.append(
            [
                pltpu.make_async_copy(source.at[0, at, :], data.at[index, at, :], sems.at[index, piece])
                for index, source in enumerate(sources)
            ]
        )
        for copy in copies[-1]:
            copy.start()
    first = pl.multiple_of(part_ref[0] * LANES, LANES)
    taps_copy = pltpu.make_async_copy(f_hbm.at[pl.ds(first, LANES), :], taps, taps_sem)
    taps_copy.start()
    for piece in range(PIECES):
        for copy in copies[piece]:
            copy.wait()
        key, value, grad, query = [
            data[index, pl.ds(piece * LANES, LANES), :].astype(jnp.float32) for index in range(4)
        ]
        out_ref[pl.ds(piece, CHANNELS, stride=ROWS_IN), :] = (key * value).T
        out_ref[pl.ds(PIECES + piece, CHANNELS, stride=ROWS_IN), :] = (grad * query).T
    taps_copy.wait()
    out_ref[pl.ds(2 * PIECES, CHANNELS, stride=ROWS_IN), :] = taps[...].T


def halves(value, axis):
    high = value.astype(jnp.bfloat16)
    low = (value - high.astype(jnp.float32)).astype(jnp.bfloat16)
    return jnp.concatenate([high, low, high], axis=axis)


def dot(left, right):
    return jnp.dot(left, right, preferred_element_type=jnp.float32)


def fft_kernel(in_ref, outer_ref, inner_ref, inner_back_ref, back_ref, twiddle_ref, out_ref):
    cos_t = twiddle_ref[0]
    sin_t = twiddle_ref[1]

    def load(base):
        return jnp.concatenate(
            [in_ref[pl.ds(base + piece, OWNERS, stride=ROWS_IN), :] for piece in range(PIECES)], axis=0
        )

    def outer(signals):
        first = dot(outer_ref[...], halves(jnp.concatenate(signals, axis=1), 0))
        turned = []
        for index in range(len(signals)):
            at = slice(index * LANES, (index + 1) * LANES)
            real, imag = first[:HALF, at], first[HALF:, at]
            turned.append(
                jnp.concatenate([real * cos_t + imag * sin_t, imag * cos_t - real * sin_t], axis=1)
            )
        return turned

    def inner(blocks, table_ref):
        return dot(halves(jnp.concatenate(blocks, axis=0), 1), table_ref[...])

    def outer_back(rows):
        turned = []
        for index in range(rows.shape[0] // HALF):
            at = slice(index * HALF, (index + 1) * HALF)
            real, imag = rows[at, :LANES], rows[at, LANES:]
            turned.append(
                jnp.concatenate([real * cos_t - imag * sin_t, imag * cos_t + real * sin_t], axis=0)
            )
        return dot(back_ref[...], halves(jnp.concatenate(turned, axis=1), 0))

    def store(result, base):
        for piece in range(PIECES):
            out_ref[pl.ds(base + piece, OWNERS, stride=ROWS_OUT), :] = result[
                piece * OWNERS : (piece + 1) * OWNERS, :
            ]

    taps = jnp.concatenate(
        [
            in_ref[pl.ds(2 * piece * OWNERS * ROWS_IN + 2 * PIECES, OWNERS, stride=ROWS_IN), :]
            for piece in range(PIECES)
        ],
        axis=0,
    )
    lag_real = jnp.zeros((HALF, LANES), jnp.float32)
    lag_imag = jnp.zeros((HALF, LANES), jnp.float32)
    starts = range(0, SEQS, GROUP)
    groups = []
    for start in starts:
        turned = []
        for seq in range(start, start + GROUP):
            base = seq * OWNERS * ROWS_IN
            turned += outer([load(base), load(base + PIECES)])
        groups.append(turned)
    groups[0] += outer([taps])
    spectra = [inner(turned, inner_ref) for turned in groups]
    taps_spec = spectra[0][2 * GROUP * HALF :]
    taps_real, taps_imag = taps_spec[:, :LANES], taps_spec[:, LANES:]
    groups = []
    for spec in spectra:
        products = []
        for index in range(GROUP):
            at = slice(2 * index * HALF, (2 * index + 1) * HALF)
            mixed_real, mixed_imag = spec[at, :LANES], spec[at, LANES:]
            at = slice((2 * index + 1) * HALF, (2 * index + 2) * HALF)
            gated_real, gated_imag = spec[at, :LANES], spec[at, LANES:]
            products.append(
                jnp.concatenate(
                    [
                        taps_real * mixed_real - taps_imag * mixed_imag,
                        taps_real * mixed_imag + taps_imag * mixed_real,
                    ],
                    axis=1,
                )
            )
            products.append(
                jnp.concatenate(
                    [
                        taps_real * gated_real + taps_imag * gated_imag,
                        taps_real * gated_imag - taps_imag * gated_real,
                    ],
                    axis=1,
                )
            )
            lag_real = lag_real + (mixed_real * gated_real + mixed_imag * gated_imag)
            lag_imag = lag_imag + (mixed_real * gated_imag - mixed_imag * gated_real)
        groups.append(products)
    groups[-1].append(jnp.concatenate([lag_real, lag_imag], axis=1))
    row_groups = [inner(products, inner_back_ref) for products in groups]
    for start, rows in zip(starts, row_groups):
        for index in range(GROUP):
            result = outer_back(rows[2 * index * HALF : 2 * (index + 1) * HALF])
            base = (start + index) * OWNERS * ROWS_OUT
            store(result[:, :LANES], base)
            store(result[:, LANES:], base + PIECES)
    lag = outer_back(row_groups[-1][2 * GROUP * HALF :])
    for seq in range(SEQS):
        store(lag, seq * OWNERS * ROWS_OUT + 2 * PIECES)


def post_kernel(
    c_ref, q_ref, k_ref, v_ref, u_ref, o_hbm, qg_hbm, kg_hbm, vg_hbm, fg_hbm, small, large, sems, large_sems
):
    copies = []
    for piece in range(PIECES):
        at = pl.ds(piece * LANES, LANES)
        conv = c_ref[pl.ds(piece, CHANNELS, stride=ROWS_OUT), :].T
        back = c_ref[pl.ds(PIECES + piece, CHANNELS, stride=ROWS_OUT), :].T
        large[at, :] = c_ref[pl.ds(2 * PIECES + piece, CHANNELS, stride=ROWS_OUT), :].T
        pieces = (
            (q_ref, conv, o_hbm),
            (u_ref, conv, qg_hbm),
            (v_ref, back, kg_hbm),
            (k_ref, back, vg_hbm),
        )
        for index, (factor, result, target) in enumerate(pieces):
            small[index, at, :] = (factor[0, at, :].astype(jnp.float32) * result).astype(jnp.bfloat16)
            copies.append(
                pltpu.make_async_copy(small.at[index, at, :], target.at[0, at, :], sems.at[index, piece])
            )
            copies[-1].start()
        copies.append(pltpu.make_async_copy(large.at[at, :], fg_hbm.at[at, :], large_sems.at[piece]))
        copies[-1].start()
    for copy in copies:
        copy.wait()


def params():
    return pltpu.CompilerParams(vmem_limit_bytes=VMEM_LIMIT)


def pre(part, *arrays):
    arrays = [pltpu.with_memory_space_constraint(array, pltpu.HBM) for array in arrays]
    return pl.pallas_call(
        pre_kernel,
        out_shape=jax.ShapeDtypeStruct((CHANNELS * ROWS_IN, LANES), jnp.float32),
        in_specs=[pl.BlockSpec(memory_space=pltpu.SMEM)] + [pl.BlockSpec(memory_space=pltpu.HBM)] * 5,
        out_specs=pl.BlockSpec(memory_space=pltpu.VMEM),
        scratch_shapes=[
            pltpu.VMEM((4, BLOCK, CHANNELS), jnp.bfloat16),
            pltpu.VMEM((LANES, CHANNELS), jnp.float32),
            pltpu.SemaphoreType.DMA((4, PIECES)),
            pltpu.SemaphoreType.DMA,
        ],
        compiler_params=params(),
    )(part, *arrays)


def transform(arrived, tables):
    return pl.pallas_call(
        fft_kernel,
        out_shape=jax.ShapeDtypeStruct((SEQS * OWNERS * ROWS_OUT, LANES), jnp.float32),
        compiler_params=params(),
    )(arrived, *tables)


def post(returned, query_seq, key_seq, value_seq, upstream):
    half = jax.ShapeDtypeStruct((1, BLOCK, CHANNELS), jnp.bfloat16)
    return pl.pallas_call(
        post_kernel,
        out_shape=(half, half, half, half, jax.ShapeDtypeStruct((BLOCK, CHANNELS), jnp.float32)),
        in_specs=[pl.BlockSpec(memory_space=pltpu.VMEM)] * 5,
        out_specs=[pl.BlockSpec(memory_space=pltpu.HBM)] * 5,
        scratch_shapes=[
            pltpu.VMEM((4, BLOCK, CHANNELS), jnp.bfloat16),
            pltpu.VMEM((BLOCK, CHANNELS), jnp.float32),
            pltpu.SemaphoreType.DMA((4, PIECES)),
            pltpu.SemaphoreType.DMA((PIECES,)),
        ],
        compiler_params=params(),
    )(returned, query_seq, key_seq, value_seq, upstream)


def exchange(rows, depth):
    shaped = rows.reshape(CHANNELS, depth, 1, LANES)
    moved = lax.all_to_all(shaped, ("dp", "seq"), split_axis=0, concat_axis=0, tiled=True)
    return moved.reshape(CHANNELS * depth, LANES)


def local(query_seq, key_seq, value_seq, upstream, filter_param):
    tables = [jnp.asarray(table) for table in constants()]
    part = lax.div(lax.axis_index("dp"), 2).astype(jnp.int32).reshape(1)
    sent = pre(part, query_seq, key_seq, value_seq, upstream, filter_param)
    arrived = exchange(sent, ROWS_IN)
    results = transform(arrived, tables)
    returned = exchange(results, ROWS_OUT)
    return post(returned, query_seq, key_seq, value_seq, upstream)


def solution(mesh):
    in_specs = (
        P("dp", "seq", None),
        P("dp", "seq", None),
        P("dp", "seq", None),
        P("dp", "seq", None),
        P("seq", None),
    )
    out_specs = (
        P("dp", "seq", None),
        P("dp", "seq", None),
        P("dp", "seq", None),
        P("dp", "seq", None),
        P("seq", None),
    )
    return jax.shard_map(local, mesh=mesh, in_specs=in_specs, out_specs=out_specs, check_vma=False)
```

```python
import math

import jax
import jax.numpy as jnp
import ml_dtypes
import numpy as np
from jax import lax
from jax.experimental import pallas as pl
from jax.experimental.pallas import tpu as pltpu
from jax.sharding import PartitionSpec as P

LANES = 128
BLOCK = 512
CHANNELS = 256
SEQS = 8
OWNERS = 32
PIECES = BLOCK // LANES
ROWS_IN = 2 * PIECES + 1
ROWS_OUT = 2 * PIECES + 1
HALF = 128
LENGTH = 2 * BLOCK * OWNERS
GROUP = 2
VMEM_LIMIT = 32 << 20


def split_parts(values):
    high = values.astype(np.float32).astype(ml_dtypes.bfloat16)
    low = (values - high.astype(np.float64)).astype(np.float32).astype(ml_dtypes.bfloat16)
    return high, low


def constants():
    freq = np.arange(HALF, dtype=np.int64)
    rows = np.arange(HALF, dtype=np.int64)
    coarse = (rows % OWNERS) * PIECES + rows // OWNERS
    turn = 2.0 * np.pi * (np.outer(2 * freq + 1, coarse) % (4 * HALF)) / (4 * HALF)
    outer = np.concatenate([np.cos(turn), -np.sin(turn)], axis=0)
    outer_high, outer_low = split_parts(outer)
    outer_cat = np.concatenate([outer_high, outer_high, outer_low], axis=1)
    scale = 2.0 / LENGTH / math.sqrt(LENGTH // 2)
    back_outer = outer.T * scale
    back_high, back_low = split_parts(back_outer)
    back_cat = np.concatenate([back_high, back_high, back_low], axis=1)
    lanes = np.arange(LANES, dtype=np.int64)
    inner_turn = 2.0 * np.pi * (np.outer(lanes, lanes) % LANES) / LANES
    cos_in, sin_in = np.cos(inner_turn), np.sin(inner_turn)
    inner = np.block([[cos_in, -sin_in], [sin_in, cos_in]])
    inner_high, inner_low = split_parts(inner)
    inner_cat = np.concatenate([inner_high, inner_high, inner_low], axis=0)
    inner_back = np.concatenate([inner_high.T, inner_high.T, inner_low.T], axis=0)
    twist = 2.0 * np.pi * np.outer(2 * freq + 1, lanes) / (2 * LENGTH)
    twiddle = np.stack([np.cos(twist), np.sin(twist)]).astype(np.float32)
    return (outer_cat, inner_cat, inner_back, back_cat, twiddle)


def pre_kernel(part_ref, q_hbm, k_hbm, v_hbm, u_hbm, f_hbm, out_ref, data, taps, sems, taps_sem):
    sources = (k_hbm, v_hbm, u_hbm, q_hbm)
    copies = []
    for piece in range(PIECES):
        at = pl.ds(piece * LANES, LANES)
        copies.append(
            [
                pltpu.make_async_copy(source.at[0, at, :], data.at[index, at, :], sems.at[index, piece])
                for index, source in enumerate(sources)
            ]
        )
        for copy in copies[-1]:
            copy.start()
    first = pl.multiple_of(part_ref[0] * LANES, LANES)
    taps_copy = pltpu.make_async_copy(f_hbm.at[pl.ds(first, LANES), :], taps, taps_sem)
    taps_copy.start()
    for piece in range(PIECES):
        for copy in copies[piece]:
            copy.wait()
        key, value, grad, query = [
            data[index, pl.ds(piece * LANES, LANES), :].astype(jnp.float32) for index in range(4)
        ]
        out_ref[pl.ds(piece, CHANNELS, stride=ROWS_IN), :] = (key * value).T
        out_ref[pl.ds(PIECES + piece, CHANNELS, stride=ROWS_IN), :] = (grad * query).T
    taps_copy.wait()
    out_ref[pl.ds(2 * PIECES, CHANNELS, stride=ROWS_IN), :] = taps[...].T


def halves(value, axis):
    high = value.astype(jnp.bfloat16)
    low = (value - high.astype(jnp.float32)).astype(jnp.bfloat16)
    return jnp.concatenate([high, low, high], axis=axis)


def dot(left, right):
    return jnp.dot(left, right, preferred_element_type=jnp.float32)


def fft_kernel(in_ref, outer_ref, inner_ref, inner_back_ref, back_ref, twiddle_ref, out_ref):
    cos_t = twiddle_ref[0]
    sin_t = twiddle_ref[1]

    def load(base):
        return jnp.concatenate(
            [in_ref[pl.ds(base + piece, OWNERS, stride=ROWS_IN), :] for piece in range(PIECES)], axis=0
        )

    def outer(signals):
        first = dot(outer_ref[...], halves(jnp.concatenate(signals, axis=1), 0))
        turned = []
        for index in range(len(signals)):
            at = slice(index * LANES, (index + 1) * LANES)
            real, imag = first[:HALF, at], first[HALF:, at]
            turned.append(
                jnp.concatenate([real * cos_t + imag * sin_t, imag * cos_t - real * sin_t], axis=1)
            )
        return turned

    def inner(blocks, table_ref):
        return dot(halves(jnp.concatenate(blocks, axis=0), 1), table_ref[...])

    def outer_back(rows):
        turned = []
        for index in range(rows.shape[0] // HALF):
            at = slice(index * HALF, (index + 1) * HALF)
            real, imag = rows[at, :LANES], rows[at, LANES:]
            turned.append(
                jnp.concatenate([real * cos_t - imag * sin_t, imag * cos_t + real * sin_t], axis=0)
            )
        return dot(back_ref[...], halves(jnp.concatenate(turned, axis=1), 0))

    def store(result, base):
        for piece in range(PIECES):
            out_ref[pl.ds(base + piece, OWNERS, stride=ROWS_OUT), :] = result[
                piece * OWNERS : (piece + 1) * OWNERS, :
            ]

    taps = jnp.concatenate(
        [
            in_ref[pl.ds(2 * piece * OWNERS * ROWS_IN + 2 * PIECES, OWNERS, stride=ROWS_IN), :]
            for piece in range(PIECES)
        ],
        axis=0,
    )
    lag_real = jnp.zeros((HALF, LANES), jnp.float32)
    lag_imag = jnp.zeros((HALF, LANES), jnp.float32)
    starts = range(0, SEQS, GROUP)
    groups = []
    for start in starts:
        turned = []
        for seq in range(start, start + GROUP):
            base = seq * OWNERS * ROWS_IN
            turned += outer([load(base), load(base + PIECES)])
        groups.append(turned)
    groups[0] += outer([taps])
    spectra = [inner(turned, inner_ref) for turned in groups]
    taps_spec = spectra[0][2 * GROUP * HALF :]
    taps_real, taps_imag = taps_spec[:, :LANES], taps_spec[:, LANES:]
    groups = []
    for spec in spectra:
        products = []
        for index in range(GROUP):
            at = slice(2 * index * HALF, (2 * index + 1) * HALF)
            mixed_real, mixed_imag = spec[at, :LANES], spec[at, LANES:]
            at = slice((2 * index + 1) * HALF, (2 * index + 2) * HALF)
            gated_real, gated_imag = spec[at, :LANES], spec[at, LANES:]
            products.append(
                jnp.concatenate(
                    [
                        taps_real * mixed_real - taps_imag * mixed_imag,
                        taps_real * mixed_imag + taps_imag * mixed_real,
                    ],
                    axis=1,
                )
            )
            products.append(
                jnp.concatenate(
                    [
                        taps_real * gated_real + taps_imag * gated_imag,
                        taps_real * gated_imag - taps_imag * gated_real,
                    ],
                    axis=1,
                )
            )
            lag_real = lag_real + (mixed_real * gated_real + mixed_imag * gated_imag)
            lag_imag = lag_imag + (mixed_real * gated_imag - mixed_imag * gated_real)
        groups.append(products)
    groups[-1].append(jnp.concatenate([lag_real, lag_imag], axis=1))
    row_groups = [inner(products, inner_back_ref) for products in groups]
    for start, rows in zip(starts, row_groups):
        for index in range(GROUP):
            result = outer_back(rows[2 * index * HALF : 2 * (index + 1) * HALF])
            base = (start + index) * OWNERS * ROWS_OUT
            store(result[:, :LANES], base)
            store(result[:, LANES:], base + PIECES)
    lag = outer_back(row_groups[-1][2 * GROUP * HALF :])
    for seq in range(SEQS):
        piece = seq % PIECES
        base = seq * OWNERS * ROWS_OUT + 2 * PIECES
        out_ref[pl.ds(base, OWNERS, stride=ROWS_OUT), :] = lag[piece * OWNERS : (piece + 1) * OWNERS, :]


def post_kernel(c_ref, q_ref, k_ref, v_ref, u_ref, o_hbm, qg_hbm, kg_hbm, vg_hbm, small, sems):
    copies = []
    for piece in range(PIECES):
        at = pl.ds(piece * LANES, LANES)
        conv = c_ref[pl.ds(piece, CHANNELS, stride=ROWS_OUT), :].T
        back = c_ref[pl.ds(PIECES + piece, CHANNELS, stride=ROWS_OUT), :].T
        pieces = (
            (q_ref, conv, o_hbm),
            (u_ref, conv, qg_hbm),
            (v_ref, back, kg_hbm),
            (k_ref, back, vg_hbm),
        )
        for index, (factor, result, target) in enumerate(pieces):
            small[index, at, :] = (factor[0, at, :].astype(jnp.float32) * result).astype(jnp.bfloat16)
            copies.append(
                pltpu.make_async_copy(small.at[index, at, :], target.at[0, at, :], sems.at[index, piece])
            )
            copies[-1].start()
    for copy in copies:
        copy.wait()


def quarter_kernel(c_ref, out_ref):
    out_ref[...] = c_ref[pl.ds(2 * PIECES, CHANNELS, stride=ROWS_OUT), :].T


def place_kernel(part_ref, *refs):
    quarters, fg_hbm, sems = refs[:PIECES], refs[PIECES], refs[PIECES + 1]
    copies = []
    for other, quarter in enumerate(quarters):
        first = pl.multiple_of(lax.bitwise_xor(part_ref[1], other) * LANES, LANES)
        copies.append(pltpu.make_async_copy(quarter, fg_hbm.at[pl.ds(first, LANES), :], sems.at[other]))
        copies[-1].start()
    for copy in copies:
        copy.wait()


def params():
    return pltpu.CompilerParams(vmem_limit_bytes=VMEM_LIMIT)


def pre(part, *arrays):
    arrays = [pltpu.with_memory_space_constraint(array, pltpu.HBM) for array in arrays]
    return pl.pallas_call(
        pre_kernel,
        out_shape=jax.ShapeDtypeStruct((CHANNELS * ROWS_IN, LANES), jnp.float32),
        in_specs=[pl.BlockSpec(memory_space=pltpu.SMEM)] + [pl.BlockSpec(memory_space=pltpu.HBM)] * 5,
        out_specs=pl.BlockSpec(memory_space=pltpu.VMEM),
        scratch_shapes=[
            pltpu.VMEM((4, BLOCK, CHANNELS), jnp.bfloat16),
            pltpu.VMEM((LANES, CHANNELS), jnp.float32),
            pltpu.SemaphoreType.DMA((4, PIECES)),
            pltpu.SemaphoreType.DMA,
        ],
        compiler_params=params(),
    )(part, *arrays)


def transform(arrived, tables):
    return pl.pallas_call(
        fft_kernel,
        out_shape=jax.ShapeDtypeStruct((SEQS * OWNERS * ROWS_OUT, LANES), jnp.float32),
        compiler_params=params(),
    )(arrived, *tables)


def post(returned, query_seq, key_seq, value_seq, upstream):
    half = jax.ShapeDtypeStruct((1, BLOCK, CHANNELS), jnp.bfloat16)
    return pl.pallas_call(
        post_kernel,
        out_shape=(half, half, half, half),
        in_specs=[pl.BlockSpec(memory_space=pltpu.VMEM)] * 5,
        out_specs=[pl.BlockSpec(memory_space=pltpu.HBM)] * 4,
        scratch_shapes=[
            pltpu.VMEM((4, BLOCK, CHANNELS), jnp.bfloat16),
            pltpu.SemaphoreType.DMA((4, PIECES)),
        ],
        cost_estimate=pl.CostEstimate(flops=2 << 20, bytes_accessed=4 << 20, transcendentals=0),
        compiler_params=params(),
    )(returned, query_seq, key_seq, value_seq, upstream)


def quarter_of(returned):
    return pl.pallas_call(
        quarter_kernel,
        out_shape=jax.ShapeDtypeStruct((LANES, CHANNELS), jnp.float32),
        in_specs=[pl.BlockSpec(memory_space=pltpu.VMEM)],
        out_specs=pl.BlockSpec(memory_space=pltpu.VMEM),
        compiler_params=params(),
    )(returned)


def place(part, quarters):
    return pl.pallas_call(
        place_kernel,
        out_shape=jax.ShapeDtypeStruct((BLOCK, CHANNELS), jnp.float32),
        in_specs=[pl.BlockSpec(memory_space=pltpu.SMEM)] + [pl.BlockSpec(memory_space=pltpu.VMEM)] * PIECES,
        out_specs=pl.BlockSpec(memory_space=pltpu.HBM),
        scratch_shapes=[pltpu.SemaphoreType.DMA((PIECES,))],
        compiler_params=params(),
    )(part, *quarters)


def exchange(rows, depth):
    shaped = rows.reshape(CHANNELS, depth, 1, LANES)
    moved = lax.all_to_all(shaped, ("dp", "seq"), split_axis=0, concat_axis=0, tiled=True)
    return moved.reshape(CHANNELS * depth, LANES)


def local(query_seq, key_seq, value_seq, upstream, filter_param):
    tables = [jnp.asarray(table) for table in constants()]
    row = lax.axis_index("dp")
    part = jnp.stack([lax.div(row, 2), lax.rem(row, PIECES)]).astype(jnp.int32)
    sent = pre(part, query_seq, key_seq, value_seq, upstream, filter_param)
    arrived = exchange(sent, ROWS_IN)
    results = transform(arrived, tables)
    returned = exchange(results, ROWS_OUT)
    mine = quarter_of(returned)
    quarters = [mine]
    for other in range(1, PIECES):
        quarters.append(lax.ppermute(mine, "dp", [(device, device ^ other) for device in range(SEQS)]))
    outputs = post(returned, query_seq, key_seq, value_seq, upstream)
    return (*outputs, place(part, quarters))


def solution(mesh):
    in_specs = (
        P("dp", "seq", None),
        P("dp", "seq", None),
        P("dp", "seq", None),
        P("dp", "seq", None),
        P("seq", None),
    )
    out_specs = (
        P("dp", "seq", None),
        P("dp", "seq", None),
        P("dp", "seq", None),
        P("dp", "seq", None),
        P("seq", None),
    )
    return jax.shard_map(local, mesh=mesh, in_specs=in_specs, out_specs=out_specs, check_vma=False)
```

```python
import math

import jax
import jax.numpy as jnp
import ml_dtypes
import numpy as np
from jax import lax
from jax.experimental import pallas as pl
from jax.experimental.pallas import tpu as pltpu
from jax.sharding import PartitionSpec as P

LANES = 128
BLOCK = 512
CHANNELS = 256
SEQS = 8
OWNERS = 32
PIECES = BLOCK // LANES
ROWS_IN = 2 * PIECES + 1
ROWS_OUT = 3 * PIECES
HALF = 128
LENGTH = 2 * BLOCK * OWNERS
GROUP = 2
VMEM_LIMIT = 32 << 20


def split_parts(values):
    high = values.astype(np.float32).astype(ml_dtypes.bfloat16)
    low = (values - high.astype(np.float64)).astype(np.float32).astype(ml_dtypes.bfloat16)
    return high, low


def constants():
    freq = np.arange(HALF, dtype=np.int64)
    rows = np.arange(HALF, dtype=np.int64)
    coarse = (rows % OWNERS) * PIECES + rows // OWNERS
    turn = 2.0 * np.pi * (np.outer(2 * freq + 1, coarse) % (4 * HALF)) / (4 * HALF)
    outer = np.concatenate([np.cos(turn), -np.sin(turn)], axis=0)
    outer_high, outer_low = split_parts(outer)
    outer_cat = np.concatenate([outer_high, outer_high, outer_low], axis=1)
    scale = 2.0 / LENGTH / math.sqrt(LENGTH // 2)
    back_outer = outer.T * scale
    back_high, back_low = split_parts(back_outer)
    back_cat = np.concatenate([back_high, back_high, back_low], axis=1)
    lanes = np.arange(LANES, dtype=np.int64)
    inner_turn = 2.0 * np.pi * (np.outer(lanes, lanes) % LANES) / LANES
    cos_in, sin_in = np.cos(inner_turn), np.sin(inner_turn)
    inner = np.block([[cos_in, -sin_in], [sin_in, cos_in]])
    inner_high, inner_low = split_parts(inner)
    inner_cat = np.concatenate([inner_high, inner_high, inner_low], axis=0)
    inner_back = np.concatenate([inner_high.T, inner_high.T, inner_low.T], axis=0)
    twist = 2.0 * np.pi * np.outer(2 * freq + 1, lanes) / (2 * LENGTH)
    twiddle = np.stack([np.cos(twist), np.sin(twist)]).astype(np.float32)
    return (outer_cat, inner_cat, inner_back, back_cat, twiddle)


def pre_kernel(q_hbm, k_hbm, v_hbm, u_hbm, f_hbm, out_ref, data, taps, sems, taps_sem):
    sources = (k_hbm, v_hbm, u_hbm, q_hbm)
    copies = []
    for piece in range(PIECES):
        at = pl.ds(piece * LANES, LANES)
        copies.append(
            [
                pltpu.make_async_copy(source.at[0, at, :], data.at[index, at, :], sems.at[index, piece])
                for index, source in enumerate(sources)
            ]
        )
        for copy in copies[-1]:
            copy.start()
    first = pl.multiple_of(lax.div(lax.axis_index("dp"), 2) * LANES, LANES)
    taps_copy = pltpu.make_async_copy(f_hbm.at[pl.ds(first, LANES), :], taps, taps_sem)
    taps_copy.start()
    for piece in range(PIECES):
        for copy in copies[piece]:
            copy.wait()
        key, value, grad, query = [
            data[index, pl.ds(piece * LANES, LANES), :].astype(jnp.float32) for index in range(4)
        ]
        out_ref[pl.ds(piece, CHANNELS, stride=ROWS_IN), :] = (key * value).T
        out_ref[pl.ds(PIECES + piece, CHANNELS, stride=ROWS_IN), :] = (grad * query).T
    taps_copy.wait()
    out_ref[pl.ds(2 * PIECES, CHANNELS, stride=ROWS_IN), :] = taps[...].T


def halves(value, axis):
    high = value.astype(jnp.bfloat16)
    low = (value - high.astype(jnp.float32)).astype(jnp.bfloat16)
    return jnp.concatenate([high, low, high], axis=axis)


def dot(left, right):
    return jnp.dot(left, right, preferred_element_type=jnp.float32)


def fft_kernel(in_ref, outer_ref, inner_ref, inner_back_ref, back_ref, twiddle_ref, out_ref):
    cos_t = twiddle_ref[0]
    sin_t = twiddle_ref[1]

    def load(base):
        return jnp.concatenate(
            [in_ref[pl.ds(base + piece, OWNERS, stride=ROWS_IN), :] for piece in range(PIECES)], axis=0
        )

    def outer(signals):
        first = dot(outer_ref[...], halves(jnp.concatenate(signals, axis=1), 0))
        turned = []
        for index in range(len(signals)):
            at = slice(index * LANES, (index + 1) * LANES)
            real, imag = first[:HALF, at], first[HALF:, at]
            turned.append(
                jnp.concatenate([real * cos_t + imag * sin_t, imag * cos_t - real * sin_t], axis=1)
            )
        return turned

    def inner(blocks, table_ref):
        return dot(halves(jnp.concatenate(blocks, axis=0), 1), table_ref[...])

    def outer_back(rows):
        turned = []
        for index in range(rows.shape[0] // HALF):
            at = slice(index * HALF, (index + 1) * HALF)
            real, imag = rows[at, :LANES], rows[at, LANES:]
            turned.append(
                jnp.concatenate([real * cos_t - imag * sin_t, imag * cos_t + real * sin_t], axis=0)
            )
        return dot(back_ref[...], halves(jnp.concatenate(turned, axis=1), 0))

    def store(result, base):
        for piece in range(PIECES):
            out_ref[pl.ds(base + piece, OWNERS, stride=ROWS_OUT), :] = result[
                piece * OWNERS : (piece + 1) * OWNERS, :
            ]

    taps = jnp.concatenate(
        [
            in_ref[pl.ds(2 * piece * OWNERS * ROWS_IN + 2 * PIECES, OWNERS, stride=ROWS_IN), :]
            for piece in range(PIECES)
        ],
        axis=0,
    )
    lag_real = jnp.zeros((HALF, LANES), jnp.float32)
    lag_imag = jnp.zeros((HALF, LANES), jnp.float32)
    starts = range(0, SEQS, GROUP)
    groups = []
    for start in starts:
        turned = []
        for seq in range(start, start + GROUP):
            base = seq * OWNERS * ROWS_IN
            turned += outer([load(base), load(base + PIECES)])
        groups.append(turned)
    groups[0] += outer([taps])
    spectra = [inner(turned, inner_ref) for turned in groups]
    taps_spec = spectra[0][2 * GROUP * HALF :]
    taps_real, taps_imag = taps_spec[:, :LANES], taps_spec[:, LANES:]
    groups = []
    for spec in spectra:
        products = []
        for index in range(GROUP):
            at = slice(2 * index * HALF, (2 * index + 1) * HALF)
            mixed_real, mixed_imag = spec[at, :LANES], spec[at, LANES:]
            at = slice((2 * index + 1) * HALF, (2 * index + 2) * HALF)
            gated_real, gated_imag = spec[at, :LANES], spec[at, LANES:]
            products.append(
                jnp.concatenate(
                    [
                        taps_real * mixed_real - taps_imag * mixed_imag,
                        taps_real * mixed_imag + taps_imag * mixed_real,
                    ],
                    axis=1,
                )
            )
            products.append(
                jnp.concatenate(
                    [
                        taps_real * gated_real + taps_imag * gated_imag,
                        taps_real * gated_imag - taps_imag * gated_real,
                    ],
                    axis=1,
                )
            )
            lag_real = lag_real + (mixed_real * gated_real + mixed_imag * gated_imag)
            lag_imag = lag_imag + (mixed_real * gated_imag - mixed_imag * gated_real)
        groups.append(products)
    groups[-1].append(jnp.concatenate([lag_real, lag_imag], axis=1))
    row_groups = [inner(products, inner_back_ref) for products in groups]
    for start, rows in zip(starts, row_groups):
        for index in range(GROUP):
            result = outer_back(rows[2 * index * HALF : 2 * (index + 1) * HALF])
            base = (start + index) * OWNERS * ROWS_OUT
            store(result[:, :LANES], base)
            store(result[:, LANES:], base + PIECES)
    lag = outer_back(row_groups[-1][2 * GROUP * HALF :])
    for seq in range(SEQS):
        store(lag, seq * OWNERS * ROWS_OUT + 2 * PIECES)


def post_kernel(
    c_ref, q_ref, k_ref, v_ref, u_ref, o_hbm, qg_hbm, kg_hbm, vg_hbm, fg_hbm, small, large, sems, large_sems
):
    copies = []
    for piece in range(PIECES):
        at = pl.ds(piece * LANES, LANES)
        conv = c_ref[pl.ds(piece, CHANNELS, stride=ROWS_OUT), :].T
        back = c_ref[pl.ds(PIECES + piece, CHANNELS, stride=ROWS_OUT), :].T
        large[at, :] = c_ref[pl.ds(2 * PIECES + piece, CHANNELS, stride=ROWS_OUT), :].T
        pieces = (
            (q_ref, conv, o_hbm),
            (u_ref, conv, qg_hbm),
            (v_ref, back, kg_hbm),
            (k_ref, back, vg_hbm),
        )
        for index, (factor, result, target) in enumerate(pieces):
            small[index, at, :] = (factor[0, at, :].astype(jnp.float32) * result).astype(jnp.bfloat16)
            copies.append(
                pltpu.make_async_copy(small.at[index, at, :], target.at[0, at, :], sems.at[index, piece])
            )
            copies[-1].start()
        copies.append(pltpu.make_async_copy(large.at[at, :], fg_hbm.at[at, :], large_sems.at[piece]))
        copies[-1].start()
    for copy in copies:
        copy.wait()


def params():
    return pltpu.CompilerParams(vmem_limit_bytes=VMEM_LIMIT)


def pre(*arrays):
    arrays = [pltpu.with_memory_space_constraint(array, pltpu.HBM) for array in arrays]
    return pl.pallas_call(
        pre_kernel,
        out_shape=jax.ShapeDtypeStruct((CHANNELS * ROWS_IN, LANES), jnp.float32),
        in_specs=[pl.BlockSpec(memory_space=pltpu.HBM)] * 5,
        out_specs=pl.BlockSpec(memory_space=pltpu.VMEM),
        scratch_shapes=[
            pltpu.VMEM((4, BLOCK, CHANNELS), jnp.bfloat16),
            pltpu.VMEM((LANES, CHANNELS), jnp.float32),
            pltpu.SemaphoreType.DMA((4, PIECES)),
            pltpu.SemaphoreType.DMA,
        ],
        compiler_params=params(),
    )(*arrays)


def transform(arrived, tables):
    return pl.pallas_call(
        fft_kernel,
        out_shape=jax.ShapeDtypeStruct((SEQS * OWNERS * ROWS_OUT, LANES), jnp.float32),
        compiler_params=params(),
    )(arrived, *tables)


def post(returned, query_seq, key_seq, value_seq, upstream):
    half = jax.ShapeDtypeStruct((1, BLOCK, CHANNELS), jnp.bfloat16)
    return pl.pallas_call(
        post_kernel,
        out_shape=(half, half, half, half, jax.ShapeDtypeStruct((BLOCK, CHANNELS), jnp.float32)),
        in_specs=[pl.BlockSpec(memory_space=pltpu.VMEM)] * 5,
        out_specs=[pl.BlockSpec(memory_space=pltpu.HBM)] * 5,
        scratch_shapes=[
            pltpu.VMEM((4, BLOCK, CHANNELS), jnp.bfloat16),
            pltpu.VMEM((BLOCK, CHANNELS), jnp.float32),
            pltpu.SemaphoreType.DMA((4, PIECES)),
            pltpu.SemaphoreType.DMA((PIECES,)),
        ],
        compiler_params=params(),
    )(returned, query_seq, key_seq, value_seq, upstream)


def exchange(rows, depth):
    shaped = rows.reshape(CHANNELS, depth, 1, LANES)
    moved = lax.all_to_all(shaped, ("dp", "seq"), split_axis=0, concat_axis=0, tiled=True)
    return moved.reshape(CHANNELS * depth, LANES)


def local(query_seq, key_seq, value_seq, upstream, filter_param):
    tables = [jnp.asarray(table) for table in constants()]
    sent = pre(query_seq, key_seq, value_seq, upstream, filter_param)
    arrived = exchange(sent, ROWS_IN)
    results = transform(arrived, tables)
    returned = exchange(results, ROWS_OUT)
    return post(returned, query_seq, key_seq, value_seq, upstream)


def solution(mesh):
    in_specs = (
        P("dp", "seq", None),
        P("dp", "seq", None),
        P("dp", "seq", None),
        P("dp", "seq", None),
        P("seq", None),
    )
    out_specs = (
        P("dp", "seq", None),
        P("dp", "seq", None),
        P("dp", "seq", None),
        P("dp", "seq", None),
        P("seq", None),
    )
    return jax.shard_map(local, mesh=mesh, in_specs=in_specs, out_specs=out_specs, check_vma=False)
```

```python
import math

import jax
import jax.numpy as jnp
import ml_dtypes
import numpy as np
from jax import lax
from jax.experimental import pallas as pl
from jax.experimental.pallas import tpu as pltpu
from jax.sharding import PartitionSpec as P

LANES = 128
BLOCK = 512
CHANNELS = 256
SEQS = 8
OWNERS = 32
PIECES = BLOCK // LANES
CHIPS = OWNERS // 2
PLACES = SEQS * CHIPS
ROWS_ONE = 2 * PIECES
ROWS_IN = 2 * ROWS_ONE + 1
ROWS_SWAP = ROWS_ONE + 1
TAPS = BLOCK // SEQS
ROWS_OUT = 3 * PIECES
HALF = 128
LENGTH = 2 * BLOCK * OWNERS
GROUP = 2
VMEM_LIMIT = 32 << 20


def split_parts(values):
    high = values.astype(np.float32).astype(ml_dtypes.bfloat16)
    low = (values - high.astype(np.float64)).astype(np.float32).astype(ml_dtypes.bfloat16)
    return high, low


def constants():
    freq = np.arange(HALF, dtype=np.int64)
    rows = np.arange(HALF, dtype=np.int64)
    coarse = (rows % OWNERS) * PIECES + rows // OWNERS
    turn = 2.0 * np.pi * (np.outer(2 * freq + 1, coarse) % (4 * HALF)) / (4 * HALF)
    back_outer = np.concatenate([np.cos(turn), -np.sin(turn)], axis=0).T
    owner = (rows % CHIPS) * 2 + rows % OWNERS // CHIPS
    coarse = owner * PIECES + rows // OWNERS
    turn = 2.0 * np.pi * (np.outer(2 * freq + 1, coarse) % (4 * HALF)) / (4 * HALF)
    outer = np.concatenate([np.cos(turn), -np.sin(turn)], axis=0)
    outer_high, outer_low = split_parts(outer)
    outer_cat = np.concatenate([outer_high, outer_high, outer_low], axis=1)
    scale = 2.0 / LENGTH / math.sqrt(LENGTH // 2)
    back_high, back_low = split_parts(back_outer * scale)
    back_cat = np.concatenate([back_high, back_high, back_low], axis=1)
    lanes = np.arange(LANES, dtype=np.int64)
    inner_turn = 2.0 * np.pi * (np.outer(lanes, lanes) % LANES) / LANES
    cos_in, sin_in = np.cos(inner_turn), np.sin(inner_turn)
    inner = np.block([[cos_in, -sin_in], [sin_in, cos_in]])
    inner_high, inner_low = split_parts(inner)
    inner_cat = np.concatenate([inner_high, inner_high, inner_low], axis=0)
    inner_back = np.concatenate([inner_high.T, inner_high.T, inner_low.T], axis=0)
    twist = 2.0 * np.pi * np.outer(2 * freq + 1, lanes) / (2 * LENGTH)
    twiddle = np.stack([np.cos(twist), np.sin(twist)]).astype(np.float32)
    return (outer_cat, inner_cat, inner_back, back_cat, twiddle)


def pre_kernel(q_hbm, k_hbm, v_hbm, u_hbm, f_hbm, out_ref, data, taps, sems, taps_sem):
    sources = (k_hbm, v_hbm, u_hbm, q_hbm)
    copies = []
    for piece in range(PIECES):
        at = pl.ds(piece * LANES, LANES)
        copies.append(
            [
                pltpu.make_async_copy(source.at[0, at, :], data.at[index, at, :], sems.at[index, piece])
                for index, source in enumerate(sources)
            ]
        )
        for copy in copies[-1]:
            copy.start()
    first = pl.multiple_of(lax.axis_index("dp") * TAPS, TAPS)
    taps_copy = pltpu.make_async_copy(f_hbm.at[pl.ds(first, TAPS), :], taps, taps_sem)
    taps_copy.start()
    even = lax.axis_index("core") == 0

    def store(rows, row):
        lower, upper = rows[:PLACES], rows[PLACES:]
        out_ref[pl.ds(row, PLACES, stride=ROWS_IN), :] = jnp.where(even, lower, upper)
        out_ref[pl.ds(ROWS_ONE + row, PLACES, stride=ROWS_IN), :] = jnp.where(even, upper, lower)

    for piece in range(PIECES):
        for copy in copies[piece]:
            copy.wait()
        key, value, grad, query = [
            data[index, pl.ds(piece * LANES, LANES), :].astype(jnp.float32) for index in range(4)
        ]
        store((key * value).T, piece)
        store((grad * query).T, PIECES + piece)
    taps_copy.wait()
    lower, upper = taps[:, :PLACES], taps[:, PLACES:]
    both = jnp.concatenate([jnp.where(even, lower, upper), jnp.where(even, upper, lower)], axis=0)
    out_ref[pl.ds(2 * ROWS_ONE, PLACES, stride=ROWS_IN), :] = both.T


def other_kernel(in_ref, out_ref):
    for row in range(ROWS_SWAP):
        out_ref[pl.ds(row, PLACES, stride=ROWS_SWAP), :] = in_ref[
            pl.ds(ROWS_ONE + row, PLACES, stride=ROWS_IN), :
        ]


def halves(value, axis):
    high = value.astype(jnp.bfloat16)
    low = (value - high.astype(jnp.float32)).astype(jnp.bfloat16)
    return jnp.concatenate([high, low, high], axis=axis)


def dot(left, right):
    return jnp.dot(left, right, preferred_element_type=jnp.float32)


def fft_kernel(in_ref, swap_ref, outer_ref, inner_ref, inner_back_ref, back_ref, twiddle_ref, out_ref):
    cos_t = twiddle_ref[0]
    sin_t = twiddle_ref[1]

    even = lax.axis_index("core") == 0

    def by_core(mine, other):
        return [jnp.where(even, mine, other), jnp.where(even, other, mine)]

    def load(seq, first):
        rows = []
        for piece in range(first, first + PIECES):
            mine = in_ref[pl.ds(seq * CHIPS * ROWS_IN + piece, CHIPS, stride=ROWS_IN), :]
            other = swap_ref[pl.ds(seq * CHIPS * ROWS_SWAP + piece, CHIPS, stride=ROWS_SWAP), :]
            rows += by_core(mine, other)
        return jnp.concatenate(rows, axis=0)

    def load_taps():
        lower = lax.broadcasted_iota(jnp.int32, (CHIPS, LANES), 1) < TAPS
        rows = []
        for piece in range(PIECES):
            mine, other = [], []
            for seq in (2 * piece, 2 * piece + 1):
                mine.append(in_ref[pl.ds(seq * CHIPS * ROWS_IN + 2 * ROWS_ONE, CHIPS, stride=ROWS_IN), :])
                other.append(
                    swap_ref[pl.ds(seq * CHIPS * ROWS_SWAP + ROWS_ONE, CHIPS, stride=ROWS_SWAP), :]
                )
            rows += by_core(
                jnp.where(lower, mine[0], pltpu.roll(mine[1], TAPS, 1)),
                jnp.where(lower, pltpu.roll(other[0], TAPS, 1), other[1]),
            )
        return jnp.concatenate(rows, axis=0)

    def outer(signals):
        first = dot(outer_ref[...], halves(jnp.concatenate(signals, axis=1), 0))
        turned = []
        for index in range(len(signals)):
            at = slice(index * LANES, (index + 1) * LANES)
            real, imag = first[:HALF, at], first[HALF:, at]
            turned.append(
                jnp.concatenate([real * cos_t + imag * sin_t, imag * cos_t - real * sin_t], axis=1)
            )
        return turned

    def inner(blocks, table_ref):
        return dot(halves(jnp.concatenate(blocks, axis=0), 1), table_ref[...])

    def outer_back(rows):
        turned = []
        for index in range(rows.shape[0] // HALF):
            at = slice(index * HALF, (index + 1) * HALF)
            real, imag = rows[at, :LANES], rows[at, LANES:]
            turned.append(
                jnp.concatenate([real * cos_t - imag * sin_t, imag * cos_t + real * sin_t], axis=0)
            )
        return dot(back_ref[...], halves(jnp.concatenate(turned, axis=1), 0))

    def store(result, base):
        for piece in range(PIECES):
            out_ref[pl.ds(base + piece, OWNERS, stride=ROWS_OUT), :] = result[
                piece * OWNERS : (piece + 1) * OWNERS, :
            ]

    lag_real = jnp.zeros((HALF, LANES), jnp.float32)
    lag_imag = jnp.zeros((HALF, LANES), jnp.float32)
    starts = range(0, SEQS, GROUP)
    groups = []
    for start in starts:
        turned = []
        for seq in range(start, start + GROUP):
            turned += outer([load(seq, 0), load(seq, PIECES)])
        groups.append(turned)
    groups[0] += outer([load_taps()])
    spectra = [inner(turned, inner_ref) for turned in groups]
    taps_spec = spectra[0][2 * GROUP * HALF :]
    taps_real, taps_imag = taps_spec[:, :LANES], taps_spec[:, LANES:]
    groups = []
    for spec in spectra:
        products = []
        for index in range(GROUP):
            at = slice(2 * index * HALF, (2 * index + 1) * HALF)
            mixed_real, mixed_imag = spec[at, :LANES], spec[at, LANES:]
            at = slice((2 * index + 1) * HALF, (2 * index + 2) * HALF)
            gated_real, gated_imag = spec[at, :LANES], spec[at, LANES:]
            products.append(
                jnp.concatenate(
                    [
                        taps_real * mixed_real - taps_imag * mixed_imag,
                        taps_real * mixed_imag + taps_imag * mixed_real,
                    ],
                    axis=1,
                )
            )
            products.append(
                jnp.concatenate(
                    [
                        taps_real * gated_real + taps_imag * gated_imag,
                        taps_real * gated_imag - taps_imag * gated_real,
                    ],
                    axis=1,
                )
            )
            lag_real = lag_real + (mixed_real * gated_real + mixed_imag * gated_imag)
            lag_imag = lag_imag + (mixed_real * gated_imag - mixed_imag * gated_real)
        groups.append(products)
    groups[-1].append(jnp.concatenate([lag_real, lag_imag], axis=1))
    row_groups = [inner(products, inner_back_ref) for products in groups]
    for start, rows in zip(starts, row_groups):
        for index in range(GROUP):
            result = outer_back(rows[2 * index * HALF : 2 * (index + 1) * HALF])
            base = (start + index) * OWNERS * ROWS_OUT
            store(result[:, :LANES], base)
            store(result[:, LANES:], base + PIECES)
    lag = outer_back(row_groups[-1][2 * GROUP * HALF :])
    for seq in range(SEQS):
        store(lag, seq * OWNERS * ROWS_OUT + 2 * PIECES)


def post_kernel(
    c_ref, q_ref, k_ref, v_ref, u_ref, o_hbm, qg_hbm, kg_hbm, vg_hbm, fg_hbm, small, large, sems, large_sems
):
    def arrived(row):
        cores = [
            c_ref[pl.ds(core * ROWS_OUT + row, PLACES, stride=2 * ROWS_OUT), :] for core in range(2)
        ]
        return jnp.concatenate(cores, axis=0).T

    copies = []
    for piece in range(PIECES):
        at = pl.ds(piece * LANES, LANES)
        conv = arrived(piece)
        back = arrived(PIECES + piece)
        large[at, :] = arrived(2 * PIECES + piece)
        pieces = (
            (q_ref, conv, o_hbm),
            (u_ref, conv, qg_hbm),
            (v_ref, back, kg_hbm),
            (k_ref, back, vg_hbm),
        )
        for index, (factor, result, target) in enumerate(pieces):
            small[index, at, :] = (factor[0, at, :].astype(jnp.float32) * result).astype(jnp.bfloat16)
            copies.append(
                pltpu.make_async_copy(small.at[index, at, :], target.at[0, at, :], sems.at[index, piece])
            )
            copies[-1].start()
        copies.append(pltpu.make_async_copy(large.at[at, :], fg_hbm.at[at, :], large_sems.at[piece]))
        copies[-1].start()
    for copy in copies:
        copy.wait()


def params():
    return pltpu.CompilerParams(vmem_limit_bytes=VMEM_LIMIT)


def pre(*arrays):
    arrays = [pltpu.with_memory_space_constraint(array, pltpu.HBM) for array in arrays]
    return pl.pallas_call(
        pre_kernel,
        out_shape=jax.ShapeDtypeStruct((PLACES * ROWS_IN, LANES), jnp.float32),
        in_specs=[pl.BlockSpec(memory_space=pltpu.HBM)] * 5,
        out_specs=pl.BlockSpec(memory_space=pltpu.VMEM),
        scratch_shapes=[
            pltpu.VMEM((4, BLOCK, CHANNELS), jnp.bfloat16),
            pltpu.VMEM((TAPS, CHANNELS), jnp.float32),
            pltpu.SemaphoreType.DMA((4, PIECES)),
            pltpu.SemaphoreType.DMA,
        ],
        compiler_params=params(),
    )(*arrays)


def other_half(arrived):
    return pl.pallas_call(
        other_kernel,
        out_shape=jax.ShapeDtypeStruct((PLACES * ROWS_SWAP, LANES), jnp.float32),
        compiler_params=params(),
    )(arrived)


def transform(arrived, swapped, tables):
    return pl.pallas_call(
        fft_kernel,
        out_shape=jax.ShapeDtypeStruct((SEQS * OWNERS * ROWS_OUT, LANES), jnp.float32),
        compiler_params=params(),
    )(arrived, swapped, *tables)


def post(returned, query_seq, key_seq, value_seq, upstream):
    half = jax.ShapeDtypeStruct((1, BLOCK, CHANNELS), jnp.bfloat16)
    return pl.pallas_call(
        post_kernel,
        out_shape=(half, half, half, half, jax.ShapeDtypeStruct((BLOCK, CHANNELS), jnp.float32)),
        in_specs=[pl.BlockSpec(memory_space=pltpu.VMEM)] * 5,
        out_specs=[pl.BlockSpec(memory_space=pltpu.HBM)] * 5,
        scratch_shapes=[
            pltpu.VMEM((4, BLOCK, CHANNELS), jnp.bfloat16),
            pltpu.VMEM((BLOCK, CHANNELS), jnp.float32),
            pltpu.SemaphoreType.DMA((4, PIECES)),
            pltpu.SemaphoreType.DMA((PIECES,)),
        ],
        compiler_params=params(),
    )(returned, query_seq, key_seq, value_seq, upstream)


def exchange(rows, axes, count):
    shaped = rows.reshape(count, rows.shape[0] // count, 1, LANES)
    moved = lax.all_to_all(shaped, axes, split_axis=0, concat_axis=0, tiled=True)
    return moved.reshape(rows.shape)


def local(query_seq, key_seq, value_seq, upstream, filter_param):
    tables = [jnp.asarray(table) for table in constants()]
    sent = pre(query_seq, key_seq, value_seq, upstream, filter_param)
    arrived = exchange(sent, ("dp", "chip"), PLACES)
    swapped = lax.ppermute(other_half(arrived), "core", [(0, 1), (1, 0)])
    results = transform(arrived, swapped, tables)
    returned = exchange(results, ("dp", "chip", "core"), CHANNELS)
    return post(returned, query_seq, key_seq, value_seq, upstream)


def solution(mesh):
    by_chip = jax.sharding.Mesh(mesh.devices.reshape(SEQS, CHIPS, 2), ("dp", "chip", "core"))
    whole = P("dp", ("chip", "core"), None)
    taps = P(("chip", "core"), None)
    return jax.shard_map(
        local,
        mesh=by_chip,
        in_specs=(whole, whole, whole, whole, taps),
        out_specs=(whole, whole, whole, whole, taps),
        check_vma=False,
    )
```

```python
import math

import jax
import jax.numpy as jnp
import ml_dtypes
import numpy as np
from jax import lax
from jax.experimental import pallas as pl
from jax.experimental.pallas import tpu as pltpu
from jax.sharding import PartitionSpec as P

LANES = 128
BLOCK = 512
CHANNELS = 256
SEQS = 8
OWNERS = 32
PIECES = BLOCK // LANES
ROWS_IN = 2 * PIECES + 1
ROWS_OUT = 2 * PIECES
Z_CHIPS = 8
HALF = 128
LENGTH = 2 * BLOCK * OWNERS
GROUP = 2
VMEM_LIMIT = 32 << 20


def split_parts(values):
    high = values.astype(np.float32).astype(ml_dtypes.bfloat16)
    low = (values - high.astype(np.float64)).astype(np.float32).astype(ml_dtypes.bfloat16)
    return high, low


def constants():
    freq = np.arange(HALF, dtype=np.int64)
    rows = np.arange(HALF, dtype=np.int64)
    coarse = (rows % OWNERS) * PIECES + rows // OWNERS
    turn = 2.0 * np.pi * (np.outer(2 * freq + 1, coarse) % (4 * HALF)) / (4 * HALF)
    outer = np.concatenate([np.cos(turn), -np.sin(turn)], axis=0)
    outer_high, outer_low = split_parts(outer)
    outer_cat = np.concatenate([outer_high, outer_high, outer_low], axis=1)
    scale = 2.0 / LENGTH / math.sqrt(LENGTH // 2)
    back_outer = outer.T * scale
    back_high, back_low = split_parts(back_outer)
    back_cat = np.concatenate([back_high, back_high, back_low], axis=1)
    lanes = np.arange(LANES, dtype=np.int64)
    inner_turn = 2.0 * np.pi * (np.outer(lanes, lanes) % LANES) / LANES
    cos_in, sin_in = np.cos(inner_turn), np.sin(inner_turn)
    inner = np.block([[cos_in, -sin_in], [sin_in, cos_in]])
    inner_high, inner_low = split_parts(inner)
    inner_cat = np.concatenate([inner_high, inner_high, inner_low], axis=0)
    inner_back = np.concatenate([inner_high.T, inner_high.T, inner_low.T], axis=0)
    twist = 2.0 * np.pi * np.outer(2 * freq + 1, lanes) / (2 * LENGTH)
    twiddle = np.stack([np.cos(twist), np.sin(twist)]).astype(np.float32)
    return (outer_cat, inner_cat, inner_back, back_cat, twiddle)


def pre_kernel(q_hbm, k_hbm, v_hbm, u_hbm, f_hbm, out_ref, data, taps, sems, taps_sem):
    sources = (k_hbm, v_hbm, u_hbm, q_hbm)
    copies = []
    for piece in range(PIECES):
        at = pl.ds(piece * LANES, LANES)
        copies.append(
            [
                pltpu.make_async_copy(source.at[0, at, :], data.at[index, at, :], sems.at[index, piece])
                for index, source in enumerate(sources)
            ]
        )
        for copy in copies[-1]:
            copy.start()
    first = pl.multiple_of(lax.div(lax.axis_index("dp"), 2) * LANES, LANES)
    taps_copy = pltpu.make_async_copy(f_hbm.at[pl.ds(first, LANES), :], taps, taps_sem)
    taps_copy.start()
    for piece in range(PIECES):
        for copy in copies[piece]:
            copy.wait()
        key, value, grad, query = [
            data[index, pl.ds(piece * LANES, LANES), :].astype(jnp.float32) for index in range(4)
        ]
        out_ref[pl.ds(piece, CHANNELS, stride=ROWS_IN), :] = (key * value).T
        out_ref[pl.ds(PIECES + piece, CHANNELS, stride=ROWS_IN), :] = (grad * query).T
    taps_copy.wait()
    out_ref[pl.ds(2 * PIECES, CHANNELS, stride=ROWS_IN), :] = taps[...].T


def halves(value, axis):
    high = value.astype(jnp.bfloat16)
    low = (value - high.astype(jnp.float32)).astype(jnp.bfloat16)
    return jnp.concatenate([high, low, high], axis=axis)


def dot(left, right):
    return jnp.dot(left, right, preferred_element_type=jnp.float32)


def turn(real, imag, cos_t, sin_t, axis):
    return jnp.concatenate([real * cos_t + imag * sin_t, imag * cos_t - real * sin_t], axis=axis)


def inner(blocks, table_ref):
    return dot(halves(jnp.concatenate(blocks, axis=0), 1), table_ref[...])


def outer_back(rows, twiddle_ref, back_ref):
    turned = [
        turn(rows[at : at + HALF, :LANES], rows[at : at + HALF, LANES:], twiddle_ref[0], -twiddle_ref[1], 0)
        for at in range(0, rows.shape[0], HALF)
    ]
    return dot(back_ref[...], halves(jnp.concatenate(turned, axis=1), 0))


def forward_kernel(
    in_ref, outer_ref, inner_ref, inner_back_ref, back_ref, twiddle_ref, spec_ref, taps_ref, lag_ref, blocks
):
    def load(base):
        return jnp.concatenate(
            [in_ref[pl.ds(base + piece, OWNERS, stride=ROWS_IN), :] for piece in range(PIECES)], axis=0
        )

    def outer(signals):
        first = dot(outer_ref[...], halves(jnp.concatenate(signals, axis=1), 0))
        return [
            turn(first[:HALF, at : at + LANES], first[HALF:, at : at + LANES], twiddle_ref[0], twiddle_ref[1], 1)
            for at in range(0, first.shape[1], LANES)
        ]

    taps = jnp.concatenate(
        [
            in_ref[pl.ds(2 * piece * OWNERS * ROWS_IN + 2 * PIECES, OWNERS, stride=ROWS_IN), :]
            for piece in range(PIECES)
        ],
        axis=0,
    )
    groups = []
    for start in range(0, SEQS, GROUP):
        turned = []
        for seq in range(start, start + GROUP):
            base = seq * OWNERS * ROWS_IN
            turned += outer([load(base), load(base + PIECES)])
        groups.append(turned)
    groups[-1] += outer([taps])
    lag_real = jnp.zeros((HALF, LANES), jnp.float32)
    lag_imag = jnp.zeros((HALF, LANES), jnp.float32)
    spectra = [inner(turned, inner_ref) for turned in groups]
    for number, spec in enumerate(spectra):
        size = 2 * GROUP * HALF
        spec_ref[number * size : (number + 1) * size, :] = spec[:size]
        for index in range(GROUP):
            at = slice(2 * index * HALF, (2 * index + 1) * HALF)
            mixed_real, mixed_imag = spec[at, :LANES], spec[at, LANES:]
            at = slice((2 * index + 1) * HALF, (2 * index + 2) * HALF)
            gated_real, gated_imag = spec[at, :LANES], spec[at, LANES:]
            lag_real = lag_real + (mixed_real * gated_real + mixed_imag * gated_imag)
            lag_imag = lag_imag + (mixed_real * gated_imag - mixed_imag * gated_real)
    taps_ref[...] = spectra[-1][2 * GROUP * HALF :]
    rows = inner([jnp.concatenate([lag_real, lag_imag], axis=1)], inner_back_ref)
    lag = outer_back(rows, twiddle_ref, back_ref)
    for piece in range(PIECES):
        blocks[:, piece, :] = lag[piece * OWNERS : (piece + 1) * OWNERS, :]
    for chip in range(Z_CHIPS):
        for x in range(2):
            for core in range(2):
                owner = lax.bitwise_xor(lax.axis_index("x"), x) * (2 * Z_CHIPS) + chip * 2
                lag_ref[chip * 4 + x * 2 + core] = blocks[owner + lax.bitwise_xor(lax.axis_index("core"), core)]


def inverse_kernel(spec_ref, taps_ref, inner_back_ref, back_ref, twiddle_ref, out_ref):
    taps_real, taps_imag = taps_ref[:, :LANES], taps_ref[:, LANES:]
    groups = []
    for seq in range(SEQS):
        at = pl.ds(2 * seq * HALF, HALF)
        mixed_real, mixed_imag = spec_ref[at, :LANES], spec_ref[at, LANES:]
        at = pl.ds((2 * seq + 1) * HALF, HALF)
        gated_real, gated_imag = spec_ref[at, :LANES], spec_ref[at, LANES:]
        conv = [
            taps_real * mixed_real - taps_imag * mixed_imag,
            taps_real * mixed_imag + taps_imag * mixed_real,
        ]
        back = [
            taps_real * gated_real + taps_imag * gated_imag,
            taps_real * gated_imag - taps_imag * gated_real,
        ]
        groups.append([jnp.concatenate(conv, axis=1), jnp.concatenate(back, axis=1)])
    row_groups = [inner(products, inner_back_ref) for products in groups]
    for seq, rows in enumerate(row_groups):
        result = outer_back(rows, twiddle_ref, back_ref)
        for which in range(2):
            for piece in range(PIECES):
                base = seq * OWNERS * ROWS_OUT + which * PIECES + piece
                out_ref[pl.ds(base, OWNERS, stride=ROWS_OUT), :] = result[
                    piece * OWNERS : (piece + 1) * OWNERS, which * LANES : (which + 1) * LANES
                ]


def post_kernel(c_ref, q_ref, k_ref, v_ref, u_ref, o_hbm, qg_hbm, kg_hbm, vg_hbm, small, sems):
    copies = []
    for piece in range(PIECES):
        at = pl.ds(piece * LANES, LANES)
        conv = c_ref[pl.ds(piece, CHANNELS, stride=ROWS_OUT), :].T
        back = c_ref[pl.ds(PIECES + piece, CHANNELS, stride=ROWS_OUT), :].T
        pieces = (
            (q_ref, conv, o_hbm),
            (u_ref, conv, qg_hbm),
            (v_ref, back, kg_hbm),
            (k_ref, back, vg_hbm),
        )
        for index, (factor, result, target) in enumerate(pieces):
            small[index, at, :] = (factor[0, at, :].astype(jnp.float32) * result).astype(jnp.bfloat16)
            copies.append(
                pltpu.make_async_copy(small.at[index, at, :], target.at[0, at, :], sems.at[index, piece])
            )
            copies[-1].start()
    for copy in copies:
        copy.wait()


def taps_kernel(*refs):
    sources, fg_ref, blocks = refs[:SEQS], refs[SEQS], refs[SEQS + 1]
    x_place, core_place = lax.axis_index("x"), lax.axis_index("core")
    for other, source in enumerate(sources):
        row = lax.bitwise_xor(lax.axis_index("dp"), other) * OWNERS
        for x in range(2):
            for core in range(2):
                first = row + lax.bitwise_xor(x_place, x) * (2 * Z_CHIPS) + lax.bitwise_xor(core_place, core)
                for chip in range(Z_CHIPS):
                    blocks[first + chip * 2] = source[(x * 2 + core) * Z_CHIPS + chip]
    for piece in range(PIECES):
        fg_ref[pl.ds(piece * LANES, LANES), :] = blocks[:, piece, :].T


def params():
    return pltpu.CompilerParams(vmem_limit_bytes=VMEM_LIMIT)


def pre(*arrays):
    arrays = [pltpu.with_memory_space_constraint(array, pltpu.HBM) for array in arrays]
    return pl.pallas_call(
        pre_kernel,
        out_shape=jax.ShapeDtypeStruct((CHANNELS * ROWS_IN, LANES), jnp.float32),
        in_specs=[pl.BlockSpec(memory_space=pltpu.HBM)] * 5,
        out_specs=pl.BlockSpec(memory_space=pltpu.VMEM),
        scratch_shapes=[
            pltpu.VMEM((4, BLOCK, CHANNELS), jnp.bfloat16),
            pltpu.VMEM((LANES, CHANNELS), jnp.float32),
            pltpu.SemaphoreType.DMA((4, PIECES)),
            pltpu.SemaphoreType.DMA,
        ],
        compiler_params=params(),
    )(*arrays)


def forward(arrived, tables):
    return pl.pallas_call(
        forward_kernel,
        out_shape=(
            jax.ShapeDtypeStruct((2 * SEQS * HALF, 2 * LANES), jnp.float32),
            jax.ShapeDtypeStruct((HALF, 2 * LANES), jnp.float32),
            jax.ShapeDtypeStruct((OWNERS, PIECES, LANES), jnp.float32),
        ),
        scratch_shapes=[pltpu.VMEM((OWNERS, PIECES, LANES), jnp.float32)],
        compiler_params=params(),
    )(arrived, *tables)


def inverse(spec, taps_spec, tables):
    return pl.pallas_call(
        inverse_kernel,
        out_shape=jax.ShapeDtypeStruct((SEQS * OWNERS * ROWS_OUT, LANES), jnp.float32),
        cost_estimate=pl.CostEstimate(flops=4 << 30, bytes_accessed=4 << 20, transcendentals=0),
        compiler_params=params(),
    )(spec, taps_spec, *tables[2:])


def post(returned, query_seq, key_seq, value_seq, upstream):
    half = jax.ShapeDtypeStruct((1, BLOCK, CHANNELS), jnp.bfloat16)
    return pl.pallas_call(
        post_kernel,
        out_shape=(half, half, half, half),
        in_specs=[pl.BlockSpec(memory_space=pltpu.VMEM)] * 5,
        out_specs=[pl.BlockSpec(memory_space=pltpu.HBM)] * 4,
        scratch_shapes=[
            pltpu.VMEM((4, BLOCK, CHANNELS), jnp.bfloat16),
            pltpu.SemaphoreType.DMA((4, PIECES)),
        ],
        compiler_params=params(),
    )(returned, query_seq, key_seq, value_seq, upstream)


def taps_grad(sources):
    return pl.pallas_call(
        taps_kernel,
        out_shape=jax.ShapeDtypeStruct((BLOCK, CHANNELS), jnp.float32),
        scratch_shapes=[pltpu.VMEM((CHANNELS, PIECES, LANES), jnp.float32)],
        compiler_params=params(),
    )(*sources)


def exchange(rows, depth):
    shaped = rows.reshape(CHANNELS, depth, 1, LANES)
    moved = lax.all_to_all(shaped, ("dp", "x", "z", "core"), split_axis=0, concat_axis=0, tiled=True)
    return moved.reshape(CHANNELS * depth, LANES)


def swap(value, axis, bits):
    return lax.ppermute(value, axis, [(place, place ^ bits) for place in range(lax.axis_size(axis))])


def spread(columns):
    columns = columns.reshape(Z_CHIPS, 2, 2, PIECES, LANES)
    by_x = jnp.stack([columns[:, 0], swap(columns[:, 1], "x", 1)])
    mine = jnp.stack([by_x[:, :, 0], swap(by_x[:, :, 1], "core", 1)], axis=1)
    mine = mine.reshape(OWNERS, PIECES, LANES)
    return [mine] + [swap(mine, "dp", other) for other in range(1, SEQS)]


def local(query_seq, key_seq, value_seq, upstream, filter_param):
    tables = [jnp.asarray(table) for table in constants()]
    sent = pre(query_seq, key_seq, value_seq, upstream, filter_param)
    arrived = exchange(sent, ROWS_IN)
    spec, taps_spec, lag = forward(arrived, tables)
    columns = lax.all_to_all(lag, "z", split_axis=0, concat_axis=0, tiled=True)
    results = inverse(spec, taps_spec, tables)
    results, columns = lax.optimization_barrier((results, columns))
    returned = exchange(results, ROWS_OUT)
    filter_grad = taps_grad(spread(columns))
    return (*post(returned, query_seq, key_seq, value_seq, upstream), filter_grad)


def solution(mesh):
    placed = jax.sharding.Mesh(mesh.devices.reshape(SEQS, 2, Z_CHIPS, 2), ("dp", "x", "z", "core"))
    whole = P("dp", ("x", "z", "core"), None)
    taps = P(("x", "z", "core"), None)
    return jax.shard_map(
        local,
        mesh=placed,
        in_specs=(whole, whole, whole, whole, taps),
        out_specs=(whole, whole, whole, whole, taps),
        check_vma=False,
    )
```

```python
import math

import jax
import jax.numpy as jnp
import ml_dtypes
import numpy as np
from jax import lax
from jax.experimental import pallas as pl
from jax.experimental.pallas import tpu as pltpu
from jax.sharding import PartitionSpec as P

LANES = 128
BLOCK = 512
CHANNELS = 256
SEQS = 8
OWNERS = 32
PIECES = BLOCK // LANES
ROWS_IN = 2 * PIECES + 1
ROWS_OUT = 2 * PIECES
Z_CHIPS = 8
HALF = 128
LENGTH = 2 * BLOCK * OWNERS
GROUP = 2
VMEM_LIMIT = 32 << 20


def split_parts(values):
    high = values.astype(np.float32).astype(ml_dtypes.bfloat16)
    low = (values - high.astype(np.float64)).astype(np.float32).astype(ml_dtypes.bfloat16)
    return high, low


def constants():
    freq = np.arange(HALF, dtype=np.int64)
    rows = np.arange(HALF, dtype=np.int64)
    coarse = (rows % OWNERS) * PIECES + rows // OWNERS
    turn = 2.0 * np.pi * (np.outer(2 * freq + 1, coarse) % (4 * HALF)) / (4 * HALF)
    outer = np.concatenate([np.cos(turn), -np.sin(turn)], axis=0)
    outer_high, outer_low = split_parts(outer)
    outer_cat = np.concatenate([outer_high, outer_high, outer_low], axis=1)
    scale = 2.0 / LENGTH / math.sqrt(LENGTH // 2)
    back_outer = outer.T * scale
    back_high, back_low = split_parts(back_outer)
    back_cat = np.concatenate([back_high, back_high, back_low], axis=1)
    lanes = np.arange(LANES, dtype=np.int64)
    inner_turn = 2.0 * np.pi * (np.outer(lanes, lanes) % LANES) / LANES
    cos_in, sin_in = np.cos(inner_turn), np.sin(inner_turn)
    inner = np.block([[cos_in, -sin_in], [sin_in, cos_in]])
    inner_high, inner_low = split_parts(inner)
    inner_cat = np.concatenate([inner_high, inner_high, inner_low], axis=0)
    inner_back = np.concatenate([inner_high.T, inner_high.T, inner_low.T], axis=0)
    twist = 2.0 * np.pi * np.outer(2 * freq + 1, lanes) / (2 * LENGTH)
    twiddle = np.stack([np.cos(twist), np.sin(twist)]).astype(np.float32)
    return (outer_cat, inner_cat, inner_back, back_cat, twiddle)


def pre_kernel(q_hbm, k_hbm, v_hbm, u_hbm, f_hbm, out_ref, data, taps, sems, taps_sem):
    sources = (k_hbm, v_hbm, u_hbm, q_hbm)
    copies = []
    for piece in range(PIECES):
        at = pl.ds(piece * LANES, LANES)
        copies.append(
            [
                pltpu.make_async_copy(source.at[0, at, :], data.at[index, at, :], sems.at[index, piece])
                for index, source in enumerate(sources)
            ]
        )
        for copy in copies[-1]:
            copy.start()
    first = pl.multiple_of(lax.div(lax.axis_index("dp"), 2) * LANES, LANES)
    taps_copy = pltpu.make_async_copy(f_hbm.at[pl.ds(first, LANES), :], taps, taps_sem)
    taps_copy.start()
    for piece in range(PIECES):
        for copy in copies[piece]:
            copy.wait()
        key, value, grad, query = [
            data[index, pl.ds(piece * LANES, LANES), :].astype(jnp.float32) for index in range(4)
        ]
        out_ref[pl.ds(piece, CHANNELS, stride=ROWS_IN), :] = (key * value).T
        out_ref[pl.ds(PIECES + piece, CHANNELS, stride=ROWS_IN), :] = (grad * query).T
    taps_copy.wait()
    out_ref[pl.ds(2 * PIECES, CHANNELS, stride=ROWS_IN), :] = taps[...].T


def halves(value, axis):
    high = value.astype(jnp.bfloat16)
    low = (value - high.astype(jnp.float32)).astype(jnp.bfloat16)
    return jnp.concatenate([high, low, high], axis=axis)


def dot(left, right):
    return jnp.dot(left, right, preferred_element_type=jnp.float32)


def turn(real, imag, cos_t, sin_t, axis):
    return jnp.concatenate([real * cos_t + imag * sin_t, imag * cos_t - real * sin_t], axis=axis)


def inner(blocks, table_ref):
    return dot(halves(jnp.concatenate(blocks, axis=0), 1), table_ref[...])


def outer_back(rows, twiddle_ref, back_ref):
    turned = [
        turn(rows[at : at + HALF, :LANES], rows[at : at + HALF, LANES:], twiddle_ref[0], -twiddle_ref[1], 0)
        for at in range(0, rows.shape[0], HALF)
    ]
    return dot(back_ref[...], halves(jnp.concatenate(turned, axis=1), 0))


def forward_kernel(
    in_ref, outer_ref, inner_ref, inner_back_ref, back_ref, twiddle_ref, spec_ref, taps_ref, lag_ref, blocks
):
    def load(base):
        return jnp.concatenate(
            [in_ref[pl.ds(base + piece, OWNERS, stride=ROWS_IN), :] for piece in range(PIECES)], axis=0
        )

    def outer(signals):
        first = dot(outer_ref[...], halves(jnp.concatenate(signals, axis=1), 0))
        return [
            turn(first[:HALF, at : at + LANES], first[HALF:, at : at + LANES], twiddle_ref[0], twiddle_ref[1], 1)
            for at in range(0, first.shape[1], LANES)
        ]

    taps = jnp.concatenate(
        [
            in_ref[pl.ds(2 * piece * OWNERS * ROWS_IN + 2 * PIECES, OWNERS, stride=ROWS_IN), :]
            for piece in range(PIECES)
        ],
        axis=0,
    )
    groups = []
    for start in range(0, SEQS, GROUP):
        turned = []
        for seq in range(start, start + GROUP):
            base = seq * OWNERS * ROWS_IN
            turned += outer([load(base), load(base + PIECES)])
        groups.append(turned)
    groups[-1] += outer([taps])
    lag_real = jnp.zeros((HALF, LANES), jnp.float32)
    lag_imag = jnp.zeros((HALF, LANES), jnp.float32)
    spectra = [inner(turned, inner_ref) for turned in groups]
    for number, spec in enumerate(spectra):
        size = 2 * GROUP * HALF
        spec_ref[number * size : (number + 1) * size, :] = spec[:size]
        for index in range(GROUP):
            at = slice(2 * index * HALF, (2 * index + 1) * HALF)
            mixed_real, mixed_imag = spec[at, :LANES], spec[at, LANES:]
            at = slice((2 * index + 1) * HALF, (2 * index + 2) * HALF)
            gated_real, gated_imag = spec[at, :LANES], spec[at, LANES:]
            lag_real = lag_real + (mixed_real * gated_real + mixed_imag * gated_imag)
            lag_imag = lag_imag + (mixed_real * gated_imag - mixed_imag * gated_real)
    taps_ref[...] = spectra[-1][2 * GROUP * HALF :]
    rows = inner([jnp.concatenate([lag_real, lag_imag], axis=1)], inner_back_ref)
    lag = outer_back(rows, twiddle_ref, back_ref)
    for piece in range(PIECES):
        blocks[:, piece, :] = lag[piece * OWNERS : (piece + 1) * OWNERS, :]
    for low in range(2):
        for high in range(Z_CHIPS // 2):
            for x in range(2):
                for core in range(2):
                    owner = lax.bitwise_xor(lax.axis_index("x"), x) * (2 * Z_CHIPS) + high * 4
                    owner = owner + lax.bitwise_xor(lax.axis_index("z_low"), low) * 2
                    owner = owner + lax.bitwise_xor(lax.axis_index("core"), core)
                    lag_ref[low * (OWNERS // 2) + high * 4 + x * 2 + core] = blocks[owner]


def inverse_kernel(spec_ref, taps_ref, inner_back_ref, back_ref, twiddle_ref, out_ref):
    taps_real, taps_imag = taps_ref[:, :LANES], taps_ref[:, LANES:]
    groups = []
    for seq in range(SEQS):
        at = pl.ds(2 * seq * HALF, HALF)
        mixed_real, mixed_imag = spec_ref[at, :LANES], spec_ref[at, LANES:]
        at = pl.ds((2 * seq + 1) * HALF, HALF)
        gated_real, gated_imag = spec_ref[at, :LANES], spec_ref[at, LANES:]
        conv = [
            taps_real * mixed_real - taps_imag * mixed_imag,
            taps_real * mixed_imag + taps_imag * mixed_real,
        ]
        back = [
            taps_real * gated_real + taps_imag * gated_imag,
            taps_real * gated_imag - taps_imag * gated_real,
        ]
        groups.append([jnp.concatenate(conv, axis=1), jnp.concatenate(back, axis=1)])
    row_groups = [inner(products, inner_back_ref) for products in groups]
    for seq, rows in enumerate(row_groups):
        result = outer_back(rows, twiddle_ref, back_ref)
        for which in range(2):
            for piece in range(PIECES):
                base = seq * OWNERS * ROWS_OUT + which * PIECES + piece
                out_ref[pl.ds(base, OWNERS, stride=ROWS_OUT), :] = result[
                    piece * OWNERS : (piece + 1) * OWNERS, which * LANES : (which + 1) * LANES
                ]


def post_kernel(c_ref, q_ref, k_ref, v_ref, u_ref, o_hbm, qg_hbm, kg_hbm, vg_hbm, small, sems):
    copies = []
    for piece in range(PIECES):
        at = pl.ds(piece * LANES, LANES)
        conv = c_ref[pl.ds(piece, CHANNELS, stride=ROWS_OUT), :].T
        back = c_ref[pl.ds(PIECES + piece, CHANNELS, stride=ROWS_OUT), :].T
        pieces = (
            (q_ref, conv, o_hbm),
            (u_ref, conv, qg_hbm),
            (v_ref, back, kg_hbm),
            (k_ref, back, vg_hbm),
        )
        for index, (factor, result, target) in enumerate(pieces):
            small[index, at, :] = (factor[0, at, :].astype(jnp.float32) * result).astype(jnp.bfloat16)
            copies.append(
                pltpu.make_async_copy(small.at[index, at, :], target.at[0, at, :], sems.at[index, piece])
            )
            copies[-1].start()
    for copy in copies:
        copy.wait()


def taps_kernel(*refs):
    sources, fg_ref, blocks = refs[:SEQS], refs[SEQS], refs[SEQS + 1]
    x_place, core_place = lax.axis_index("x"), lax.axis_index("core")
    for other, source in enumerate(sources):
        row = lax.bitwise_xor(lax.axis_index("dp"), other) * OWNERS
        for x in range(2):
            for core in range(2):
                first = row + lax.bitwise_xor(x_place, x) * (2 * Z_CHIPS) + lax.bitwise_xor(core_place, core)
                for high in range(Z_CHIPS // 2):
                    for low in range(2):
                        chip = high * 2 + lax.bitwise_xor(lax.axis_index("z_low"), low)
                        blocks[first + chip * 2] = source[(x * 2 + core) * Z_CHIPS + high * 2 + low]
    for piece in range(PIECES):
        fg_ref[pl.ds(piece * LANES, LANES), :] = blocks[:, piece, :].T


def params():
    return pltpu.CompilerParams(vmem_limit_bytes=VMEM_LIMIT)


def pre(*arrays):
    arrays = [pltpu.with_memory_space_constraint(array, pltpu.HBM) for array in arrays]
    return pl.pallas_call(
        pre_kernel,
        out_shape=jax.ShapeDtypeStruct((CHANNELS * ROWS_IN, LANES), jnp.float32),
        in_specs=[pl.BlockSpec(memory_space=pltpu.HBM)] * 5,
        out_specs=pl.BlockSpec(memory_space=pltpu.VMEM),
        scratch_shapes=[
            pltpu.VMEM((4, BLOCK, CHANNELS), jnp.bfloat16),
            pltpu.VMEM((LANES, CHANNELS), jnp.float32),
            pltpu.SemaphoreType.DMA((4, PIECES)),
            pltpu.SemaphoreType.DMA,
        ],
        compiler_params=params(),
    )(*arrays)


def forward(arrived, tables):
    return pl.pallas_call(
        forward_kernel,
        out_shape=(
            jax.ShapeDtypeStruct((2 * SEQS * HALF, 2 * LANES), jnp.float32),
            jax.ShapeDtypeStruct((HALF, 2 * LANES), jnp.float32),
            jax.ShapeDtypeStruct((OWNERS, PIECES, LANES), jnp.float32),
        ),
        scratch_shapes=[pltpu.VMEM((OWNERS, PIECES, LANES), jnp.float32)],
        compiler_params=params(),
    )(arrived, *tables)


def inverse(spec, taps_spec, tables):
    return pl.pallas_call(
        inverse_kernel,
        out_shape=jax.ShapeDtypeStruct((SEQS * OWNERS * ROWS_OUT, LANES), jnp.float32),
        cost_estimate=pl.CostEstimate(flops=4 << 30, bytes_accessed=4 << 20, transcendentals=0),
        compiler_params=params(),
    )(spec, taps_spec, *tables[2:])


def post(returned, query_seq, key_seq, value_seq, upstream):
    half = jax.ShapeDtypeStruct((1, BLOCK, CHANNELS), jnp.bfloat16)
    return pl.pallas_call(
        post_kernel,
        out_shape=(half, half, half, half),
        in_specs=[pl.BlockSpec(memory_space=pltpu.VMEM)] * 5,
        out_specs=[pl.BlockSpec(memory_space=pltpu.HBM)] * 4,
        scratch_shapes=[
            pltpu.VMEM((4, BLOCK, CHANNELS), jnp.bfloat16),
            pltpu.SemaphoreType.DMA((4, PIECES)),
        ],
        compiler_params=params(),
    )(returned, query_seq, key_seq, value_seq, upstream)


def taps_grad(sources):
    return pl.pallas_call(
        taps_kernel,
        out_shape=jax.ShapeDtypeStruct((BLOCK, CHANNELS), jnp.float32),
        scratch_shapes=[pltpu.VMEM((CHANNELS, PIECES, LANES), jnp.float32)],
        compiler_params=params(),
    )(*sources)


def exchange(rows, depth):
    shaped = rows.reshape(CHANNELS, depth, 1, LANES)
    moved = lax.all_to_all(shaped, ("dp", "x", "z_high", "z_low", "core"), split_axis=0, concat_axis=0, tiled=True)
    return moved.reshape(CHANNELS * depth, LANES)


def swap(value, axis, bits):
    return lax.ppermute(value, axis, [(place, place ^ bits) for place in range(lax.axis_size(axis))])


def along_z(lag):
    pair = lag.reshape(2, Z_CHIPS // 2, 4, PIECES, LANES)
    pair = jnp.stack([pair[0], swap(pair[1], "z_low", 1)], axis=1)
    return lax.all_to_all(pair, "z_high", split_axis=0, concat_axis=0, tiled=True)


def spread(columns):
    columns = columns.reshape(Z_CHIPS // 2, 2, 2, 2, PIECES, LANES)
    by_x = jnp.stack([columns[:, :, 0], swap(columns[:, :, 1], "x", 1)])
    mine = jnp.stack([by_x[:, :, :, 0], swap(by_x[:, :, :, 1], "core", 1)], axis=1)
    mine = mine.reshape(OWNERS, PIECES, LANES)
    return [mine] + [swap(mine, "dp", other) for other in range(1, SEQS)]


def local(query_seq, key_seq, value_seq, upstream, filter_param):
    tables = [jnp.asarray(table) for table in constants()]
    sent = pre(query_seq, key_seq, value_seq, upstream, filter_param)
    arrived = exchange(sent, ROWS_IN)
    spec, taps_spec, lag = forward(arrived, tables)
    columns = along_z(lag)
    results = inverse(spec, taps_spec, tables)
    results, columns = lax.optimization_barrier((results, columns))
    returned = exchange(results, ROWS_OUT)
    filter_grad = taps_grad(spread(columns))
    return (*post(returned, query_seq, key_seq, value_seq, upstream), filter_grad)


def solution(mesh):
    names = ("dp", "x", "z_high", "z_low", "core")
    placed = jax.sharding.Mesh(mesh.devices.reshape(SEQS, 2, Z_CHIPS // 2, 2, 2), names)
    whole = P("dp", names[1:], None)
    taps = P(names[1:], None)
    return jax.shard_map(
        local,
        mesh=placed,
        in_specs=(whole, whole, whole, whole, taps),
        out_specs=(whole, whole, whole, whole, taps),
        check_vma=False,
    )
```

```python
import math

import jax
import jax.numpy as jnp
import ml_dtypes
import numpy as np
from jax import lax
from jax.experimental import pallas as pl
from jax.experimental.pallas import tpu as pltpu
from jax.sharding import PartitionSpec as P

LANES = 128
BLOCK = 512
CHANNELS = 256
SEQS = 8
OWNERS = 32
PIECES = BLOCK // LANES
ROWS_IN = 2 * PIECES + 1
ROWS_OUT = 3 * PIECES
HALF = 128
LENGTH = 2 * BLOCK * OWNERS
GROUP = 1
VMEM_LIMIT = 32 << 20


def split_parts(values):
    high = values.astype(np.float32).astype(ml_dtypes.bfloat16)
    low = (values - high.astype(np.float64)).astype(np.float32).astype(ml_dtypes.bfloat16)
    return high, low


def constants():
    freq = np.arange(HALF, dtype=np.int64)
    rows = np.arange(HALF, dtype=np.int64)
    coarse = (rows % OWNERS) * PIECES + rows // OWNERS
    turn = 2.0 * np.pi * (np.outer(2 * freq + 1, coarse) % (4 * HALF)) / (4 * HALF)
    outer = np.concatenate([np.cos(turn), -np.sin(turn)], axis=0)
    outer_high, outer_low = split_parts(outer)
    outer_cat = np.concatenate([outer_high, outer_high, outer_low], axis=1)
    scale = 2.0 / LENGTH / math.sqrt(LENGTH // 2)
    back_outer = outer.T * scale
    back_high, back_low = split_parts(back_outer)
    back_cat = np.concatenate([back_high, back_high, back_low], axis=1)
    lanes = np.arange(LANES, dtype=np.int64)
    inner_turn = 2.0 * np.pi * (np.outer(lanes, lanes) % LANES) / LANES
    cos_in, sin_in = np.cos(inner_turn), np.sin(inner_turn)
    inner = np.block([[cos_in, -sin_in], [sin_in, cos_in]])
    inner_high, inner_low = split_parts(inner)
    inner_cat = np.concatenate([inner_high, inner_high, inner_low], axis=0)
    inner_back = np.concatenate([inner_high.T, inner_high.T, inner_low.T], axis=0)
    twist = 2.0 * np.pi * np.outer(2 * freq + 1, lanes) / (2 * LENGTH)
    twiddle = np.stack([np.cos(twist), np.sin(twist)]).astype(np.float32)
    return (outer_cat, inner_cat, inner_back, back_cat, twiddle)


def pre_kernel(q_hbm, k_hbm, v_hbm, u_hbm, f_hbm, out_ref, data, taps, sems, taps_sem):
    sources = (k_hbm, v_hbm, u_hbm, q_hbm)
    copies = []
    for piece in range(PIECES):
        at = pl.ds(piece * LANES, LANES)
        copies.append(
            [
                pltpu.make_async_copy(source.at[0, at, :], data.at[index, at, :], sems.at[index, piece])
                for index, source in enumerate(sources)
            ]
        )
        for copy in copies[-1]:
            copy.start()
    first = pl.multiple_of(lax.div(lax.axis_index("dp"), 2) * LANES, LANES)
    taps_copy = pltpu.make_async_copy(f_hbm.at[pl.ds(first, LANES), :], taps, taps_sem)
    taps_copy.start()
    for piece in range(PIECES):
        for copy in copies[piece]:
            copy.wait()
        key, value, grad, query = [
            data[index, pl.ds(piece * LANES, LANES), :].astype(jnp.float32) for index in range(4)
        ]
        out_ref[pl.ds(piece, CHANNELS, stride=ROWS_IN), :] = (key * value).T
        out_ref[pl.ds(PIECES + piece, CHANNELS, stride=ROWS_IN), :] = (grad * query).T
    taps_copy.wait()
    out_ref[pl.ds(2 * PIECES, CHANNELS, stride=ROWS_IN), :] = taps[...].T


def halves(value, axis):
    high = value.astype(jnp.bfloat16)
    low = (value - high.astype(jnp.float32)).astype(jnp.bfloat16)
    return jnp.concatenate([high, low, high], axis=axis)


def dot(left, right):
    return jnp.dot(left, right, preferred_element_type=jnp.float32)


def fft_kernel(in_ref, outer_ref, inner_ref, inner_back_ref, back_ref, twiddle_ref, out_ref):
    cos_t = twiddle_ref[0]
    sin_t = twiddle_ref[1]

    def load(base):
        return jnp.concatenate(
            [in_ref[pl.ds(base + piece, OWNERS, stride=ROWS_IN), :] for piece in range(PIECES)], axis=0
        )

    def outer(signals):
        first = dot(outer_ref[...], halves(jnp.concatenate(signals, axis=1), 0))
        turned = []
        for index in range(len(signals)):
            at = slice(index * LANES, (index + 1) * LANES)
            real, imag = first[:HALF, at], first[HALF:, at]
            turned.append(
                jnp.concatenate([real * cos_t + imag * sin_t, imag * cos_t - real * sin_t], axis=1)
            )
        return turned

    def inner(blocks, table_ref):
        return dot(halves(jnp.concatenate(blocks, axis=0), 1), table_ref[...])

    def outer_back(rows):
        turned = []
        for index in range(rows.shape[0] // HALF):
            at = slice(index * HALF, (index + 1) * HALF)
            real, imag = rows[at, :LANES], rows[at, LANES:]
            turned.append(
                jnp.concatenate([real * cos_t - imag * sin_t, imag * cos_t + real * sin_t], axis=0)
            )
        return dot(back_ref[...], halves(jnp.concatenate(turned, axis=1), 0))

    def store(result, base):
        for piece in range(PIECES):
            out_ref[pl.ds(base + piece, OWNERS, stride=ROWS_OUT), :] = result[
                piece * OWNERS : (piece + 1) * OWNERS, :
            ]

    taps = jnp.concatenate(
        [
            in_ref[pl.ds(2 * piece * OWNERS * ROWS_IN + 2 * PIECES, OWNERS, stride=ROWS_IN), :]
            for piece in range(PIECES)
        ],
        axis=0,
    )
    lag_real = jnp.zeros((HALF, LANES), jnp.float32)
    lag_imag = jnp.zeros((HALF, LANES), jnp.float32)
    starts = range(0, SEQS, GROUP)
    groups = []
    for start in starts:
        turned = []
        for seq in range(start, start + GROUP):
            base = seq * OWNERS * ROWS_IN
            turned += outer([load(base), load(base + PIECES)])
        groups.append(turned)
    groups[0] += outer([taps])
    spectra = [inner(turned, inner_ref) for turned in groups]
    taps_spec = spectra[0][2 * GROUP * HALF :]
    taps_real, taps_imag = taps_spec[:, :LANES], taps_spec[:, LANES:]
    groups = []
    for spec in spectra:
        products = []
        for index in range(GROUP):
            at = slice(2 * index * HALF, (2 * index + 1) * HALF)
            mixed_real, mixed_imag = spec[at, :LANES], spec[at, LANES:]
            at = slice((2 * index + 1) * HALF, (2 * index + 2) * HALF)
            gated_real, gated_imag = spec[at, :LANES], spec[at, LANES:]
            products.append(
                jnp.concatenate(
                    [
                        taps_real * mixed_real - taps_imag * mixed_imag,
                        taps_real * mixed_imag + taps_imag * mixed_real,
                    ],
                    axis=1,
                )
            )
            products.append(
                jnp.concatenate(
                    [
                        taps_real * gated_real + taps_imag * gated_imag,
                        taps_real * gated_imag - taps_imag * gated_real,
                    ],
                    axis=1,
                )
            )
            lag_real = lag_real + (mixed_real * gated_real + mixed_imag * gated_imag)
            lag_imag = lag_imag + (mixed_real * gated_imag - mixed_imag * gated_real)
        groups.append(products)
    groups[-1].append(jnp.concatenate([lag_real, lag_imag], axis=1))
    row_groups = [inner(products, inner_back_ref) for products in groups]
    for start, rows in zip(starts, row_groups):
        for index in range(GROUP):
            result = outer_back(rows[2 * index * HALF : 2 * (index + 1) * HALF])
            base = (start + index) * OWNERS * ROWS_OUT
            store(result[:, :LANES], base)
            store(result[:, LANES:], base + PIECES)
    lag = outer_back(row_groups[-1][2 * GROUP * HALF :])
    for seq in range(SEQS):
        store(lag, seq * OWNERS * ROWS_OUT + 2 * PIECES)


def post_kernel(
    c_ref, q_ref, k_ref, v_ref, u_ref, o_hbm, qg_hbm, kg_hbm, vg_hbm, fg_hbm, small, large, sems, large_sems
):
    copies = []
    for piece in range(PIECES):
        at = pl.ds(piece * LANES, LANES)
        large[at, :] = c_ref[pl.ds(2 * PIECES + piece, CHANNELS, stride=ROWS_OUT), :].T
        copies.append(pltpu.make_async_copy(large.at[at, :], fg_hbm.at[at, :], large_sems.at[piece]))
        copies[-1].start()
        conv = c_ref[pl.ds(piece, CHANNELS, stride=ROWS_OUT), :].T
        back = c_ref[pl.ds(PIECES + piece, CHANNELS, stride=ROWS_OUT), :].T
        pieces = (
            (q_ref, conv, o_hbm),
            (u_ref, conv, qg_hbm),
            (v_ref, back, kg_hbm),
            (k_ref, back, vg_hbm),
        )
        for index, (factor, result, target) in enumerate(pieces):
            small[index, at, :] = (factor[0, at, :].astype(jnp.float32) * result).astype(jnp.bfloat16)
            copies.append(
                pltpu.make_async_copy(small.at[index, at, :], target.at[0, at, :], sems.at[index, piece])
            )
            copies[-1].start()
    for copy in copies:
        copy.wait()


def params():
    return pltpu.CompilerParams(vmem_limit_bytes=VMEM_LIMIT)


def pre(*arrays):
    arrays = [pltpu.with_memory_space_constraint(array, pltpu.HBM) for array in arrays]
    return pl.pallas_call(
        pre_kernel,
        out_shape=jax.ShapeDtypeStruct((CHANNELS * ROWS_IN, LANES), jnp.float32),
        in_specs=[pl.BlockSpec(memory_space=pltpu.HBM)] * 5,
        out_specs=pl.BlockSpec(memory_space=pltpu.VMEM),
        scratch_shapes=[
            pltpu.VMEM((4, BLOCK, CHANNELS), jnp.bfloat16),
            pltpu.VMEM((LANES, CHANNELS), jnp.float32),
            pltpu.SemaphoreType.DMA((4, PIECES)),
            pltpu.SemaphoreType.DMA,
        ],
        compiler_params=params(),
    )(*arrays)


def transform(arrived, tables):
    return pl.pallas_call(
        fft_kernel,
        out_shape=jax.ShapeDtypeStruct((SEQS * OWNERS * ROWS_OUT, LANES), jnp.float32),
        compiler_params=params(),
    )(arrived, *tables)


def post(returned, query_seq, key_seq, value_seq, upstream):
    half = jax.ShapeDtypeStruct((1, BLOCK, CHANNELS), jnp.bfloat16)
    return pl.pallas_call(
        post_kernel,
        out_shape=(half, half, half, half, jax.ShapeDtypeStruct((BLOCK, CHANNELS), jnp.float32)),
        in_specs=[pl.BlockSpec(memory_space=pltpu.VMEM)] * 5,
        out_specs=[pl.BlockSpec(memory_space=pltpu.HBM)] * 5,
        scratch_shapes=[
            pltpu.VMEM((4, BLOCK, CHANNELS), jnp.bfloat16),
            pltpu.VMEM((BLOCK, CHANNELS), jnp.float32),
            pltpu.SemaphoreType.DMA((4, PIECES)),
            pltpu.SemaphoreType.DMA((PIECES,)),
        ],
        compiler_params=params(),
    )(returned, query_seq, key_seq, value_seq, upstream)


def exchange(rows, depth):
    shaped = rows.reshape(CHANNELS, depth, 1, LANES)
    moved = lax.all_to_all(shaped, ("dp", "seq"), split_axis=0, concat_axis=0, tiled=True)
    return moved.reshape(CHANNELS * depth, LANES)


def local(query_seq, key_seq, value_seq, upstream, filter_param):
    tables = [jnp.asarray(table) for table in constants()]
    sent = pre(query_seq, key_seq, value_seq, upstream, filter_param)
    arrived = exchange(sent, ROWS_IN)
    results = transform(arrived, tables)
    returned = exchange(results, ROWS_OUT)
    return post(returned, query_seq, key_seq, value_seq, upstream)


def solution(mesh):
    in_specs = (
        P("dp", "seq", None),
        P("dp", "seq", None),
        P("dp", "seq", None),
        P("dp", "seq", None),
        P("seq", None),
    )
    out_specs = (
        P("dp", "seq", None),
        P("dp", "seq", None),
        P("dp", "seq", None),
        P("dp", "seq", None),
        P("seq", None),
    )
    return jax.shard_map(local, mesh=mesh, in_specs=in_specs, out_specs=out_specs, check_vma=False)
```

```python
import math

import jax
import jax.numpy as jnp
import ml_dtypes
import numpy as np
from jax import lax
from jax.experimental import pallas as pl
from jax.experimental.pallas import tpu as pltpu
from jax.sharding import PartitionSpec as P

LANES = 128
BLOCK = 512
CHANNELS = 256
SEQS = 8
OWNERS = 32
PIECES = BLOCK // LANES
ROWS_IN = 2 * PIECES + 1
ROWS_OUT = 3 * PIECES
HALF = 128
LENGTH = 2 * BLOCK * OWNERS
GROUP = 2
VMEM_LIMIT = 32 << 20


def split_parts(values):
    high = values.astype(np.float32).astype(ml_dtypes.bfloat16)
    low = (values - high.astype(np.float64)).astype(np.float32).astype(ml_dtypes.bfloat16)
    return high, low


def constants():
    freq = np.arange(HALF, dtype=np.int64)
    rows = np.arange(HALF, dtype=np.int64)
    coarse = (rows % OWNERS) * PIECES + rows // OWNERS
    turn = 2.0 * np.pi * (np.outer(2 * freq + 1, coarse) % (4 * HALF)) / (4 * HALF)
    outer = np.concatenate([np.cos(turn), -np.sin(turn)], axis=0)
    outer_high, outer_low = split_parts(outer)
    outer_cat = np.concatenate([outer_high, outer_high, outer_low], axis=1)
    scale = 2.0 / LENGTH / math.sqrt(LENGTH // 2)
    back_outer = outer.T * scale
    back_high, back_low = split_parts(back_outer)
    back_cat = np.concatenate([back_high, back_high, back_low], axis=1)
    lanes = np.arange(LANES, dtype=np.int64)
    inner_turn = 2.0 * np.pi * (np.outer(lanes, lanes) % LANES) / LANES
    cos_in, sin_in = np.cos(inner_turn), np.sin(inner_turn)
    inner = np.block([[cos_in, -sin_in], [sin_in, cos_in]])
    inner_high, inner_low = split_parts(inner)
    inner_cat = np.concatenate([inner_high, inner_high, inner_low], axis=0)
    inner_back = np.concatenate([inner_high.T, inner_high.T, inner_low.T], axis=0)
    twist = 2.0 * np.pi * np.outer(2 * freq + 1, lanes) / (2 * LENGTH)
    twiddle = np.stack([np.cos(twist), np.sin(twist)]).astype(np.float32)
    return (outer_cat, inner_cat, inner_back, back_cat, twiddle)


def pre_kernel(q_hbm, k_hbm, v_hbm, u_hbm, f_hbm, out_ref, data, taps, sems, taps_sem):
    first = pl.multiple_of(lax.div(lax.axis_index("dp"), 2) * LANES, LANES)
    taps_copy = pltpu.make_async_copy(f_hbm.at[pl.ds(first, LANES), :], taps, taps_sem)
    taps_copy.start()
    sources = (k_hbm, v_hbm, u_hbm, q_hbm)
    copies = []
    for piece in range(PIECES):
        at = pl.ds(piece * LANES, LANES)
        copies.append(
            [
                pltpu.make_async_copy(source.at[0, at, :], data.at[index, at, :], sems.at[index, piece])
                for index, source in enumerate(sources)
            ]
        )
        for copy in copies[-1]:
            copy.start()
    for piece in range(PIECES):
        for copy in copies[piece]:
            copy.wait()
        key, value, grad, query = [
            data[index, pl.ds(piece * LANES, LANES), :].astype(jnp.float32) for index in range(4)
        ]
        out_ref[pl.ds(piece, CHANNELS, stride=ROWS_IN), :] = (key * value).T
        out_ref[pl.ds(PIECES + piece, CHANNELS, stride=ROWS_IN), :] = (grad * query).T
    taps_copy.wait()
    out_ref[pl.ds(2 * PIECES, CHANNELS, stride=ROWS_IN), :] = taps[...].T


def halves(value, axis):
    high = value.astype(jnp.bfloat16)
    low = (value - high.astype(jnp.float32)).astype(jnp.bfloat16)
    return jnp.concatenate([high, low, high], axis=axis)


def dot(left, right):
    return jnp.dot(left, right, preferred_element_type=jnp.float32)


def fft_kernel(in_ref, outer_ref, inner_ref, inner_back_ref, back_ref, twiddle_ref, out_ref):
    cos_t = twiddle_ref[0]
    sin_t = twiddle_ref[1]

    def load(base):
        return jnp.concatenate(
            [in_ref[pl.ds(base + piece, OWNERS, stride=ROWS_IN), :] for piece in range(PIECES)], axis=0
        )

    def outer(signals):
        first = dot(outer_ref[...], halves(jnp.concatenate(signals, axis=1), 0))
        turned = []
        for index in range(len(signals)):
            at = slice(index * LANES, (index + 1) * LANES)
            real, imag = first[:HALF, at], first[HALF:, at]
            turned.append(
                jnp.concatenate([real * cos_t + imag * sin_t, imag * cos_t - real * sin_t], axis=1)
            )
        return turned

    def inner(blocks, table_ref):
        return dot(halves(jnp.concatenate(blocks, axis=0), 1), table_ref[...])

    def outer_back(rows):
        turned = []
        for index in range(rows.shape[0] // HALF):
            at = slice(index * HALF, (index + 1) * HALF)
            real, imag = rows[at, :LANES], rows[at, LANES:]
            turned.append(
                jnp.concatenate([real * cos_t - imag * sin_t, imag * cos_t + real * sin_t], axis=0)
            )
        return dot(back_ref[...], halves(jnp.concatenate(turned, axis=1), 0))

    def store(result, base):
        for piece in range(PIECES):
            out_ref[pl.ds(base + piece, OWNERS, stride=ROWS_OUT), :] = result[
                piece * OWNERS : (piece + 1) * OWNERS, :
            ]

    taps = jnp.concatenate(
        [
            in_ref[pl.ds(2 * piece * OWNERS * ROWS_IN + 2 * PIECES, OWNERS, stride=ROWS_IN), :]
            for piece in range(PIECES)
        ],
        axis=0,
    )
    lag_real = jnp.zeros((HALF, LANES), jnp.float32)
    lag_imag = jnp.zeros((HALF, LANES), jnp.float32)
    starts = range(0, SEQS, GROUP)
    groups = []
    for start in starts:
        turned = []
        for seq in range(start, start + GROUP):
            base = seq * OWNERS * ROWS_IN
            turned += outer([load(base), load(base + PIECES)])
        groups.append(turned)
    groups[0] += outer([taps])
    spectra = [inner(turned, inner_ref) for turned in groups]
    taps_spec = spectra[0][2 * GROUP * HALF :]
    taps_real, taps_imag = taps_spec[:, :LANES], taps_spec[:, LANES:]
    groups = []
    for spec in spectra:
        products = []
        for index in range(GROUP):
            at = slice(2 * index * HALF, (2 * index + 1) * HALF)
            mixed_real, mixed_imag = spec[at, :LANES], spec[at, LANES:]
            at = slice((2 * index + 1) * HALF, (2 * index + 2) * HALF)
            gated_real, gated_imag = spec[at, :LANES], spec[at, LANES:]
            products.append(
                jnp.concatenate(
                    [
                        taps_real * mixed_real - taps_imag * mixed_imag,
                        taps_real * mixed_imag + taps_imag * mixed_real,
                    ],
                    axis=1,
                )
            )
            products.append(
                jnp.concatenate(
                    [
                        taps_real * gated_real + taps_imag * gated_imag,
                        taps_real * gated_imag - taps_imag * gated_real,
                    ],
                    axis=1,
                )
            )
            lag_real = lag_real + (mixed_real * gated_real + mixed_imag * gated_imag)
            lag_imag = lag_imag + (mixed_real * gated_imag - mixed_imag * gated_real)
        groups.append(products)
    groups[-1].append(jnp.concatenate([lag_real, lag_imag], axis=1))
    row_groups = [inner(products, inner_back_ref) for products in groups]
    for start, rows in zip(starts, row_groups):
        for index in range(GROUP):
            result = outer_back(rows[2 * index * HALF : 2 * (index + 1) * HALF])
            base = (start + index) * OWNERS * ROWS_OUT
            store(result[:, :LANES], base)
            store(result[:, LANES:], base + PIECES)
    lag = outer_back(row_groups[-1][2 * GROUP * HALF :])
    for seq in range(SEQS):
        store(lag, seq * OWNERS * ROWS_OUT + 2 * PIECES)


def post_kernel(
    c_ref, q_ref, k_ref, v_ref, u_ref, o_hbm, qg_hbm, kg_hbm, vg_hbm, fg_hbm, small, large, sems, large_sems
):
    copies = []
    for piece in range(PIECES):
        at = pl.ds(piece * LANES, LANES)
        conv = c_ref[pl.ds(piece, CHANNELS, stride=ROWS_OUT), :].T
        back = c_ref[pl.ds(PIECES + piece, CHANNELS, stride=ROWS_OUT), :].T
        large[at, :] = c_ref[pl.ds(2 * PIECES + piece, CHANNELS, stride=ROWS_OUT), :].T
        pieces = (
            (q_ref, conv, o_hbm),
            (u_ref, conv, qg_hbm),
            (v_ref, back, kg_hbm),
            (k_ref, back, vg_hbm),
        )
        for index, (factor, result, target) in enumerate(pieces):
            small[index, at, :] = (factor[0, at, :].astype(jnp.float32) * result).astype(jnp.bfloat16)
            copies.append(
                pltpu.make_async_copy(small.at[index, at, :], target.at[0, at, :], sems.at[index, piece])
            )
            copies[-1].start()
        copies.append(pltpu.make_async_copy(large.at[at, :], fg_hbm.at[at, :], large_sems.at[piece]))
        copies[-1].start()
    for copy in copies:
        copy.wait()


def params():
    return pltpu.CompilerParams(vmem_limit_bytes=VMEM_LIMIT)


def pre(*arrays):
    arrays = [pltpu.with_memory_space_constraint(array, pltpu.HBM) for array in arrays]
    return pl.pallas_call(
        pre_kernel,
        out_shape=jax.ShapeDtypeStruct((CHANNELS * ROWS_IN, LANES), jnp.float32),
        in_specs=[pl.BlockSpec(memory_space=pltpu.HBM)] * 5,
        out_specs=pl.BlockSpec(memory_space=pltpu.VMEM),
        scratch_shapes=[
            pltpu.VMEM((4, BLOCK, CHANNELS), jnp.bfloat16),
            pltpu.VMEM((LANES, CHANNELS), jnp.float32),
            pltpu.SemaphoreType.DMA((4, PIECES)),
            pltpu.SemaphoreType.DMA,
        ],
        compiler_params=params(),
    )(*arrays)


def transform(arrived, tables):
    return pl.pallas_call(
        fft_kernel,
        out_shape=jax.ShapeDtypeStruct((SEQS * OWNERS * ROWS_OUT, LANES), jnp.float32),
        compiler_params=params(),
    )(arrived, *tables)


def post(returned, query_seq, key_seq, value_seq, upstream):
    half = jax.ShapeDtypeStruct((1, BLOCK, CHANNELS), jnp.bfloat16)
    return pl.pallas_call(
        post_kernel,
        out_shape=(half, half, half, half, jax.ShapeDtypeStruct((BLOCK, CHANNELS), jnp.float32)),
        in_specs=[pl.BlockSpec(memory_space=pltpu.VMEM)] * 5,
        out_specs=[pl.BlockSpec(memory_space=pltpu.HBM)] * 5,
        scratch_shapes=[
            pltpu.VMEM((4, BLOCK, CHANNELS), jnp.bfloat16),
            pltpu.VMEM((BLOCK, CHANNELS), jnp.float32),
            pltpu.SemaphoreType.DMA((4, PIECES)),
            pltpu.SemaphoreType.DMA((PIECES,)),
        ],
        compiler_params=params(),
    )(returned, query_seq, key_seq, value_seq, upstream)


def exchange(rows, depth):
    shaped = rows.reshape(CHANNELS, depth, 1, LANES)
    moved = lax.all_to_all(shaped, ("dp", "seq"), split_axis=0, concat_axis=0, tiled=True)
    return moved.reshape(CHANNELS * depth, LANES)


def local(query_seq, key_seq, value_seq, upstream, filter_param):
    tables = [jnp.asarray(table) for table in constants()]
    sent = pre(query_seq, key_seq, value_seq, upstream, filter_param)
    arrived = exchange(sent, ROWS_IN)
    results = transform(arrived, tables)
    returned = exchange(results, ROWS_OUT)
    return post(returned, query_seq, key_seq, value_seq, upstream)


def solution(mesh):
    in_specs = (
        P("dp", "seq", None),
        P("dp", "seq", None),
        P("dp", "seq", None),
        P("dp", "seq", None),
        P("seq", None),
    )
    out_specs = (
        P("dp", "seq", None),
        P("dp", "seq", None),
        P("dp", "seq", None),
        P("dp", "seq", None),
        P("seq", None),
    )
    return jax.shard_map(local, mesh=mesh, in_specs=in_specs, out_specs=out_specs, check_vma=False)
```
